256 devices in a mesh: req: 64 (over x, z, core), tp: 4 (over y).
Axes of the slice: x: 4, y: 4, z: 8, core: 2. Of those that a mesh axis runs over, the one named last changes fastest.
Arguments:
- hidden_in: bfloat16 [512, 1600], P('req'), may hold values from -6 to 6
- norm_gain: float32 [1600], replicated, may hold values from 0.1 to 1.9
- query_weight: bfloat16 [1600, 1280], P(None, 'tp'), may hold values from -0.15625 to 0.15625
- memory_weight: bfloat16 [1600, 512], P(None, 'tp'), may hold values from -0.15625 to 0.15625
- attention_out: bfloat16 [1280, 1600], P('tp'), may hold values from -0.15625 to 0.15625
- attention_gain: float32 [1280], P('tp'), may hold values from 0.1 to 1.9
- mamba_input: bfloat16 [2, 1600, 1600], P(None, None, 'tp'), may hold values from -0.15625 to 0.15625
- conv_weight: float32 [4, 1600], P(None, 'tp'), may hold values from -3 to 3
- conv_state: bfloat16 [512, 3, 1600], P('req', None, 'tp'), may hold values from -6 to 6
- select_weight: bfloat16 [1600, 132], P('tp'), may hold values from -0.15625 to 0.15625
- step_weight: bfloat16 [100, 1600], P(None, 'tp'), may hold values from -0.625 to 0.625
- step_bias: float32 [1600], P('tp'), may hold values from -4 to -1
- decay_log: float32 [16, 1600], P(None, 'tp'), may hold values from 0 to 2.77
- skip_gain: float32 [1600], P('tp'), may hold values from 0.5 to 1.5
- scan_state: float32 [512, 16, 1600], P('req', None, 'tp'), may hold values from -6 to 6
- mamba_gain: float32 [1600], P('tp'), may hold values from 0.1 to 1.9
- mamba_out: bfloat16 [1600, 1600], P('tp'), may hold values from -0.15625 to 0.15625
- cache_blocks: bfloat16 [2176, 4, 512, 128], P('req', 'tp'), as said below
- lengths: int32 [512], replicated, may hold values from 257 to 8192, as said below
- slot_request: int32 [2176], P('req'), may hold values from -1 to 511, as said below
- slot_block: int32 [2176], P('req'), may hold values from 0 to 15, as said below
Outputs:
- layer_out: bfloat16 [512, 1600], P('req', 'tp')
- new_state: float32 [512, 16, 1600], P('req', None, 'tp')
The draws below stay inside these ranges and needn't reach their ends.
Inputs may be any that keep to these rules, and one draw needn't show every extreme that they name: `lengths`: some request holds exactly 8192 tokens. `slot_request`: -1 marks an empty slot; a request with L cached tokens fills exactly ceil(L / 512) slots; the slots of one index of req hold at most 2 blocks of the requests of any one index of req (requests r with equal r // 8), and some index of req holds exactly 2. `slot_block`: the slots of one request carry its block numbers 0 to ceil(L / 512) - 1, each once; empty slots carry 0. `cache_blocks`: the first 64 entries of the last dimension are keys, the rest values.
All inputs are finite; a program needn't handle non-finite values.
Results may differ from the reference program's by a relative error of at most 0.012.
Values may be sent and summed in bfloat16 or wider, within the bound.
A program may use at most 64 MiB of HBM per device.

```python
import jax
import jax.numpy as jnp
from jax import lax

D = 1600
HQ = 20
HK = 4
HD = 64
MI = 1600
NS = 16
DTR = 100
CONV = 4
BLK = 512
MAXB = 16
REQ_DEV = 8
REQUESTS = 512
POOL_DEV = 34
SLOTS = 2176


def block_plan(key):
    holders = SLOTS // POOL_DEV
    rank_span = REQUESTS - 1
    group_rank = jax.random.permutation(jax.random.fold_in(key, 35), REQ_DEV).astype(jnp.int32) + (REQUESTS - REQ_DEV)
    rest_rank = jax.random.permutation(jax.random.fold_in(key, 31), REQUESTS - REQ_DEV).astype(jnp.int32)
    rank_order = jnp.concatenate([group_rank, rest_rank]).astype(jnp.int32)
    group_shift = jax.random.randint(jax.random.fold_in(key, 36), (), 0, holders).astype(jnp.int32) * REQ_DEV
    rank_order = jnp.roll(rank_order, group_shift).astype(jnp.int32)
    rank_power = rank_order
    for repeat in range(4):
        rank_power = rank_power * rank_order // rank_span
    block_count = 1 + (MAXB - 1) * rank_power // rank_span
    last_fill = jax.random.randint(jax.random.fold_in(key, 32), (REQUESTS,), BLK // 2, BLK).astype(jnp.int32) + 1
    last_fill = jnp.where(rank_order == 0, BLK // 2 + 1, last_fill).astype(jnp.int32)
    lengths = (block_count - 1) * BLK + last_fill
    lengths = jnp.where(rank_order == rank_span, MAXB * BLK, lengths).astype(jnp.int32)
    block_count = jnp.where(rank_order == rank_span, MAXB, block_count).astype(jnp.int32)
    device_order = jax.random.permutation(jax.random.fold_in(key, 37), holders).astype(jnp.int32)
    laid_request = (device_order[:, None] * REQ_DEV + jnp.arange(REQ_DEV, dtype=jnp.int32)[None, :]).reshape(REQUESTS).astype(jnp.int32)
    laid_count = block_count[laid_request]
    laid_start = (jnp.cumsum(laid_count) - laid_count).astype(jnp.int32)
    total_blocks = jnp.sum(laid_count)
    global_block = jnp.arange(SLOTS, dtype=jnp.int32)
    rotation = ((device_order[0] - 1 + holders) % holders).astype(jnp.int32)
    slot_of = ((global_block + rotation) % holders * POOL_DEV + global_block // holders).astype(jnp.int32)
    laid_index = (jnp.sum((laid_start[None, :] <= global_block[:, None]).astype(jnp.int32), 1) - 1).astype(jnp.int32)
    owner_of = laid_request[laid_index]
    filled = global_block < total_blocks
    number_of = global_block - laid_start[laid_index]
    slot_request = jnp.zeros((SLOTS,), jnp.int32).at[slot_of].set(jnp.where(filled, owner_of, -1).astype(jnp.int32))
    slot_block = jnp.zeros((SLOTS,), jnp.int32).at[slot_of].set(jnp.where(filled, number_of, 0).astype(jnp.int32))
    return (lengths, slot_request, slot_block)


def draw_lengths(key, part):
    return block_plan(key)[0]


def draw_slot_request(key, part):
    return block_plan(key)[1]


def draw_slot_block(key, part):
    return block_plan(key)[2]


def draw_cache_blocks(key, part):
    shape = (SLOTS, HK, BLK, HD)
    base_keys = jax.random.normal(jax.random.fold_in(key, 41), shape, jnp.float32)
    base_values = jax.random.normal(jax.random.fold_in(key, 42), shape, jnp.float32)
    return jnp.concatenate([base_keys, base_values], -1).astype(jnp.bfloat16)


def shard_levels(stream_key, shape, cuts, low, top_value):
    def one(axis_at, blocks):
        draws = jax.random.uniform(jax.random.fold_in(jax.random.fold_in(stream_key, 6), axis_at), (blocks,), jnp.float32, low / len(cuts), top_value / len(cuts))
        return jnp.repeat(jnp.exp(draws), shape[axis_at] // blocks).reshape((-1,) + (1,) * (len(shape) - axis_at - 1))

    gain = one(*cuts[0])
    for cut in cuts[1:]:
        gain = gain * one(*cut)
    return gain


def noise(key, dims, width, reach, cuts=(), held_as=jnp.bfloat16):
    loudness = shard_levels(key, dims, cuts, -0.22, 0.18) if cuts else 1.0
    result = jax.random.normal(key, dims, jnp.float32) * width * loudness
    return jnp.minimum(jnp.maximum(result, -reach), reach).astype(held_as)


def setup_inputs(seed: int = 0) -> dict:
    key_of = jax.random.split(jax.random.key(seed), 22)
    hidden_in = noise(key_of[0], (REQUESTS, D), 1.0, 6.0, ((0, 64),))
    norm_gain = jnp.clip(1.0 + 0.18 * jax.random.normal(key_of[1], (D,), jnp.float32), 0.1, 1.9)
    query_weight = noise(key_of[2], (D, HQ * HD), D ** -0.5, 0.15625, ((1, 4),))
    memory_weight = noise(key_of[3], (D, HK * 2 * HD), D ** -0.5, 0.15625, ((1, 4),))
    attention_out = noise(key_of[4], (HQ * HD, D), (HQ * HD) ** -0.5, 0.15625, ((0, 4),))
    attention_gain = jnp.clip(1.0 + 0.18 * jax.random.normal(key_of[5], (HQ * HD,), jnp.float32), 0.1, 1.9)
    mamba_input = noise(key_of[6], (2, D, MI), D ** -0.5, 0.15625, ((2, 4),))
    conv_weight = noise(key_of[7], (CONV, MI), 0.5, 3.0, ((1, 4),), jnp.float32)
    conv_state = noise(key_of[8], (REQUESTS, CONV - 1, MI), 1.0, 6.0, ((0, 64), (2, 4)))
    select_weight = noise(key_of[9], (MI, DTR + 2 * NS), MI ** -0.5, 0.15625, ((0, 4),))
    step_weight = noise(key_of[10], (DTR, MI), DTR ** -0.5, 0.625, ((1, 4),))
    step_bias = jnp.clip(-4.0 + 3.0 * jax.random.uniform(key_of[11], (MI,), jnp.float32) ** shard_levels(key_of[11], (MI,), ((0, 4),), -0.2, 0.2), -4.0, -1.0)
    decay_log = jnp.clip(2.77 * jax.random.uniform(key_of[12], (NS, MI), jnp.float32) ** shard_levels(key_of[12], (NS, MI), ((1, 4),), -0.2, 0.2), 0.0, 2.77)
    skip_gain = jnp.clip(0.5 + 1.0 * jax.random.uniform(key_of[13], (MI,), jnp.float32) ** shard_levels(key_of[13], (MI,), ((0, 4),), -0.2, 0.2), 0.5, 1.5)
    scan_state = noise(key_of[14], (REQUESTS, NS, MI), 1.0, 6.0, ((0, 64), (2, 4)), jnp.float32)
    mamba_gain = jnp.clip(1.0 + 0.18 * jax.random.normal(key_of[15], (MI,), jnp.float32), 0.1, 1.9)
    mamba_out = noise(key_of[16], (MI, D), MI ** -0.5, 0.15625, ((0, 4),))
    cache_blocks = draw_cache_blocks(jax.random.fold_in(key_of[21], 71), 0)
    lengths = draw_lengths(jax.random.fold_in(key_of[21], 71), 0)
    slot_request = draw_slot_request(jax.random.fold_in(key_of[21], 71), 0)
    slot_block = draw_slot_block(jax.random.fold_in(key_of[21], 71), 0)
    return {"hidden_in": hidden_in, "norm_gain": norm_gain, "query_weight": query_weight, "memory_weight": memory_weight, "attention_out": attention_out, "attention_gain": attention_gain, "mamba_input": mamba_input, "conv_weight": conv_weight, "conv_state": conv_state, "select_weight": select_weight, "step_weight": step_weight, "step_bias": step_bias, "decay_log": decay_log, "skip_gain": skip_gain, "scan_state": scan_state, "mamba_gain": mamba_gain, "mamba_out": mamba_out, "cache_blocks": cache_blocks, "lengths": lengths, "slot_request": slot_request, "slot_block": slot_block}


def rotate_pairs(vector, position):
    head_dim = vector.shape[-1]
    half_dim = head_dim // 2
    frequency = jnp.power(jnp.float32(10000.0), -jnp.arange(half_dim, dtype=jnp.float32) * (2.0 / head_dim))
    angles = position.astype(jnp.float32)[:, None, None] * frequency
    cosine = jnp.cos(angles)
    sine_part = jnp.sin(angles)
    front_half = vector[..., :half_dim]
    back_half = vector[..., half_dim:]
    return jnp.concatenate([front_half * cosine - back_half * sine_part, back_half * cosine + front_half * sine_part], -1)

def reference(hidden_in, norm_gain, query_weight, memory_weight, attention_out, attention_gain, mamba_input, conv_weight, conv_state, select_weight, step_weight, step_bias, decay_log, skip_gain, scan_state, mamba_gain, mamba_out, cache_blocks, lengths, slot_request, slot_block):
    hidden_f = hidden_in.astype(jnp.float32)
    normed = (hidden_f * lax.rsqrt(lax.optimization_barrier(jnp.mean(hidden_f * hidden_f, -1, keepdims=True)) + 1e-06) * norm_gain).astype(jnp.bfloat16)
    group = HQ // HK
    query_raw = jnp.dot(normed, query_weight, preferred_element_type=jnp.float32).reshape(REQUESTS, HQ, HD)
    query = rotate_pairs(query_raw, lengths).astype(jnp.bfloat16)
    memory = jnp.dot(normed, memory_weight, preferred_element_type=jnp.float32).reshape(REQUESTS, HK, 2 * HD)
    key_new = rotate_pairs(memory[..., :HD], lengths).astype(jnp.bfloat16)
    value_new = memory[..., HD:].astype(jnp.bfloat16)
    slot_used = slot_request >= 0
    owner_row = jnp.where(slot_used, slot_request, 0).astype(jnp.int32)
    segment = jnp.where(slot_used, slot_request, REQUESTS).astype(jnp.int32)
    valid_len = jnp.where(slot_used, lengths[owner_row] - slot_block * BLK, 0)
    live_mask = jnp.arange(BLK)[None, :] < valid_len[:, None]
    pieces = []
    for kv_index in range(HK):
        head_query = query[owner_row][:, kv_index * group:(kv_index + 1) * group].astype(jnp.float32)
        keys = cache_blocks[:, kv_index, :, :HD].astype(jnp.float32)
        values = cache_blocks[:, kv_index, :, HD:].astype(jnp.float32)
        scores = jnp.einsum('sgd,std->sgt', head_query, keys) * HD ** (-0.5)
        scores = jnp.where(live_mask[:, None, :], scores, -1e+30)
        block_max = lax.optimization_barrier(jnp.max(scores, 2))
        weights = jnp.where(live_mask[:, None, :], jnp.exp(scores - block_max[..., None]), 0.0).astype(jnp.bfloat16)
        weights_f = weights.astype(jnp.float32)
        block_sum = lax.optimization_barrier(jnp.sum(weights_f, 2))
        block_out = jnp.einsum('sgt,std->sgd', weights_f, values)
        global_max = jax.ops.segment_max(block_max, segment, REQUESTS + 1)[:REQUESTS]
        own_query = query[:, kv_index * group:(kv_index + 1) * group].astype(jnp.float32)
        own_score = lax.optimization_barrier(jnp.sum(own_query * key_new[:, kv_index:kv_index + 1].astype(jnp.float32), -1)) * HD ** (-0.5)
        top = jnp.maximum(global_max, own_score)
        rescale = jnp.exp(block_max - top[owner_row])
        own_weight = jnp.exp(own_score - top)
        numer = jax.ops.segment_sum(block_out * rescale[..., None], segment, REQUESTS + 1)[:REQUESTS]
        numer = numer + own_weight[..., None] * value_new[:, kv_index:kv_index + 1].astype(jnp.float32)
        denom = jax.ops.segment_sum(block_sum * rescale, segment, REQUESTS + 1)[:REQUESTS] + own_weight
        pieces.append(numer / denom[..., None])
    attention = jnp.concatenate(pieces, 1).reshape(REQUESTS, HQ * HD)
    mamba_x = jnp.dot(normed, mamba_input[0], preferred_element_type=jnp.float32).astype(jnp.bfloat16)
    gate_branch = jnp.dot(normed, mamba_input[1], preferred_element_type=jnp.float32)
    conv_sum = conv_weight[CONV - 1] * mamba_x.astype(jnp.float32)
    for tap_index in range(CONV - 1):
        conv_sum = conv_sum + conv_weight[tap_index] * conv_state[:, tap_index].astype(jnp.float32)
    activated = jax.nn.silu(conv_sum).astype(jnp.bfloat16)
    selection = jnp.dot(activated, select_weight, preferred_element_type=jnp.float32)
    step_rank = selection[:, :DTR].astype(jnp.bfloat16)
    input_map = selection[:, DTR:DTR + NS]
    output_map = selection[:, DTR + NS:]
    step_size = jax.nn.softplus(jnp.dot(step_rank, step_weight, preferred_element_type=jnp.float32) + step_bias)
    active_f = activated.astype(jnp.float32)
    new_state = jnp.exp(-step_size[:, None, :] * jnp.exp(decay_log)[None]) * scan_state + step_size[:, None, :] * input_map[:, :, None] * active_f[:, None, :]
    mamba_y = (lax.optimization_barrier(jnp.sum(output_map[:, :, None] * new_state, 1)) + skip_gain * active_f) * jax.nn.silu(gate_branch)
    attn_scale = jnp.sqrt(lax.optimization_barrier(jnp.mean(attention * attention, -1)) + 1e-06)
    mamba_scale = jnp.sqrt(lax.optimization_barrier(jnp.mean(mamba_y * mamba_y, -1)) + 1e-06)
    attn_used = (attention * attention_gain).astype(jnp.bfloat16)
    mamba_used = (mamba_y * mamba_gain).astype(jnp.bfloat16)
    mixed = 0.5 * (jnp.dot(attn_used, attention_out, preferred_element_type=jnp.float32) / attn_scale[:, None] + jnp.dot(mamba_used, mamba_out, preferred_element_type=jnp.float32) / mamba_scale[:, None])
    layer_out = (hidden_f + mixed).astype(jnp.bfloat16)
    return (layer_out, new_state)
```

```python
import math

import jax
import jax.numpy as jnp
import numpy as np
from jax import lax
from jax.experimental import pallas as pl
from jax.experimental.pallas import tpu as pltpu
from jax.sharding import PartitionSpec as P

F32 = jnp.float32
BF16 = jnp.bfloat16
NEG = -1e30
ROWS = 8
HEADS = 5
HD = 64
LANES = 128
SPAD = 40
TP_COLS = 400
TP_PAD = 512
NT = (((1,), (1,)), ((), ()))


def iota(shape, axis):
    return lax.broadcasted_iota(jnp.int32, shape, axis)


def dot(a, b):
    return jnp.dot(a, b, preferred_element_type=F32)


def dot_nt(a, b):
    return lax.dot_general(a, b, NT, preferred_element_type=F32)


def silu(v):
    return v * (1.0 / (1.0 + jnp.exp(-v)))


def softplus(v):
    return jnp.maximum(v, 0.0) + jnp.log1p(jnp.exp(-jnp.abs(v)))


LOCAL = (
    "len_s", "sr_s", "sb_s", "hidden", "gain", "freq", "wq", "wm", "mi", "cw", "cs", "sw", "st", "sb", "dl", "sg",
    "ss", "mg", "mo", "cache", "ag", "wo",
)


def kernel(n, tp_n, slots, *refs):
    hbm = dict(zip(LOCAL, refs[: len(LOCAL)]))
    out_layer, out_state = refs[len(LOCAL) : len(LOCAL) + 2]
    refs = refs[len(LOCAL) + 2 :]
    ref = dict(zip(LOCAL, refs[: len(LOCAL)]))
    (
        q_all, sel_buf, msg, inbox, m_send, m_recv, a_send, a_recv, q_slot, o_slot, state_v, layer_v, y_v,
        in_sem, out_sem, send_sem, recv_sem,
    ) = refs[len(LOCAL) :]
    me = lax.axis_index("req")
    tp = lax.axis_index("tp")

    copies = {}
    for k, name in enumerate(LOCAL):
        dst = ref[name].at[pl.ds(0, HEADS * HD)] if name == "wq" else ref[name]
        copies[name] = pltpu.make_async_copy(hbm[name], dst, in_sem.at[k])
        copies[name].start()

    barrier = pltpu.get_barrier_semaphore()

    def greet(i, carry):
        pl.semaphore_signal(barrier, inc=1, device_id={"req": lax.rem(me + i, n)})
        return carry

    lax.fori_loop(1, n, greet, 0)
    for i in range(1, tp_n):
        pl.semaphore_signal(barrier, inc=1, device_id={"tp": lax.rem(tp + i, tp_n)})

    def tp_start(src, dst, k):
        for i in range(1, tp_n):
            p = lax.rem(tp + i, tp_n)
            pltpu.make_async_remote_copy(
                src_ref=src(p), dst_ref=dst.at[tp], send_sem=send_sem.at[k], recv_sem=recv_sem.at[k],
                device_id={"tp": p},
            ).start()

    def wait_all(buf, k, count, which):
        view = buf.at[pl.ds(0, count)]
        copy = pltpu.make_async_remote_copy(
            src_ref=view, dst_ref=view, send_sem=send_sem.at[k], recv_sem=recv_sem.at[k], device_id={"tp": tp}
        )
        if which == "send":
            copy.wait_send()
        else:
            copy.wait_recv()

    lane8 = iota((ROWS, LANES), 1)
    low8 = lane8 < HD

    ref["wq"][pl.ds(HEADS * HD, 64), :] = jnp.zeros((64, ref["wq"].shape[1]), BF16)
    copies["hidden"].wait()
    copies["gain"].wait()
    hidden = ref["hidden"][...].astype(F32)
    width = hidden.shape[1]
    mean = jnp.sum(hidden * hidden, axis=1, keepdims=True) * (1.0 / width)
    normed = (hidden * lax.rsqrt(mean + 1e-06) * ref["gain"][...]).astype(BF16)

    for name in ("len_s", "sr_s", "sb_s", "freq"):
        copies[name].wait()
    position = jnp.zeros((ROWS, LANES), F32)
    row8 = iota((ROWS, LANES), 0)
    for r in range(ROWS):
        position = jnp.where(row8 == r, ref["len_s"][me * ROWS + r].astype(F32), position)
    angles = position * ref["freq"][...]
    cosine = jnp.cos(angles)
    sine = jnp.sin(angles)
    front = (lane8 & (HD - 1)) < HD // 2

    def rot(v):
        other = jnp.where(front, -pltpu.roll(v, LANES - HD // 2, 1), pltpu.roll(v, HD // 2, 1))
        return v * cosine + other * sine

    copies["wq"].wait()
    q_raw = dot_nt(normed, ref["wq"][...])
    query = [rot(q_raw[:, c * LANES : (c + 1) * LANES]).astype(BF16) for c in range(3)]
    for c in range(3):
        q_all[me, :, c * LANES : (c + 1) * LANES] = query[c]

    pl.semaphore_wait(barrier, n - 1 + tp_n - 1)

    def spread(i, carry):
        pltpu.make_async_remote_copy(
            src_ref=q_all.at[me], dst_ref=q_all.at[me], send_sem=send_sem.at[0], recv_sem=recv_sem.at[0],
            device_id={"req": lax.rem(me + i, n)},
        ).start()
        return carry

    lax.fori_loop(1, n, spread, 0)

    copies["mi"].wait()
    mamba_x = dot_nt(normed, ref["mi"][0]).astype(BF16)
    for name in ("cw", "cs", "sw"):
        copies[name].wait()
    taps = ref["cw"].shape[0]
    conv = ref["cw"][taps - 1 : taps, :] * mamba_x.astype(F32)
    for j in range(taps - 1):
        conv = conv + ref["cw"][j : j + 1, :] * ref["cs"][j].astype(F32)
    activated = silu(conv).astype(BF16)
    part = dot_nt(activated, ref["sw"][...])
    sel_buf[tp] = jnp.concatenate([part, jnp.zeros((ROWS, 2 * LANES - part.shape[1]), F32)], axis=1)
    tp_start(lambda p: sel_buf.at[tp], sel_buf, 1)

    gate = silu(dot_nt(normed, ref["mi"][1]))
    copies["wm"].wait()
    memory = dot(normed, ref["wm"][...])
    key_value = jnp.where(low8, rot(memory), memory).astype(BF16).astype(F32)
    swapped = pltpu.roll(key_value, HD, 1)
    key_both = jnp.where(low8, key_value, swapped)
    value_both = jnp.where(low8, swapped, key_value)

    own_score = []
    for h in range(HEADS):
        half = low8 if h % 2 == 0 else jnp.logical_not(low8)
        prod = jnp.where(half, query[h // 2].astype(F32) * key_both, 0.0)
        own_score.append(jnp.sum(prod, axis=1, keepdims=True) * HD**-0.5)

    lane40 = lax.rem(lane8, SPAD)
    lane40 = jnp.where(lane8 < 3 * SPAD, lane40, -1)
    sr_row = jnp.full((ROWS, LANES), -1, jnp.int32)
    sub_col = iota((SPAD, LANES), 0)
    sr_col = jnp.full((SPAD, LANES), -1, jnp.int32)
    for s in range(slots):
        v = ref["sr_s"][s]
        sr_row = jnp.where(lane40 == s, v, sr_row)
        sr_col = jnp.where(sub_col == s, v, sr_col)
    dest_row = lax.shift_right_arithmetic(sr_row, 3)
    rank_row = jnp.zeros((ROWS, LANES), jnp.int32)
    for s in range(slots):
        d = lax.shift_right_arithmetic(ref["sr_s"][s], 3)
        rank_row = rank_row + jnp.where((dest_row == d) & (lane40 > s), 1, 0)
    m_rows = n * 8
    mr = iota((m_rows, LANES), 0)
    mj = lax.shift_right_arithmetic(mr & 7, 1)
    cj = jnp.where(lane8 < SPAD, 0, jnp.where(lane8 < 2 * SPAD, 1, jnp.where(lane8 < 3 * SPAD, 2, -1)))
    pick = (
        (lax.shift_right_arithmetic(mr, 3) == dest_row[0:1, :])
        & ((mr & 1) == rank_row[0:1, :])
        & (mj == cj[0:1, :])
    )
    pick = jnp.where(pick, 1.0, 0.0).astype(BF16)
    own_pick = jnp.concatenate([sr_col] * (n * 8 // LANES), axis=1) if n * 8 >= LANES else sr_col[:, 0 : n * 8]
    own_pick = jnp.where(own_pick == iota((SPAD, n * 8), 1), 1.0, 0.0).astype(BF16)

    wait_all(sel_buf, 1, tp_n - 1, "recv")
    selection = sel_buf[0]
    for p in range(1, tp_n):
        selection = selection + sel_buf[p]
    dtr = ref["st"].shape[1]
    ns = ref["dl"].shape[0]
    for name in ("st", "sb", "dl", "sg", "ss", "mg", "mo"):
        copies[name].wait()
    step = softplus(dot_nt(selection[:, 0:dtr].astype(BF16), ref["st"][...]) + ref["sb"][...])
    maps = pltpu.roll(selection, selection.shape[1] - dtr, 1)[:, 0:LANES]
    maps = jnp.transpose(maps)
    active = activated.astype(F32)
    decay = jnp.exp(ref["dl"][...])
    drive = step * active
    for r in range(ROWS):
        new = (
            jnp.exp(-step[r : r + 1, :] * decay) * ref["ss"][r]
            + drive[r : r + 1, :] * maps[0:ns, r : r + 1]
        )
        state_v[r] = new
        y_v[r : r + 1, :] = jnp.sum(maps[ns : 2 * ns, r : r + 1] * new, axis=0, keepdims=True)
    state_out = pltpu.make_async_copy(state_v, out_state, out_sem.at[0])
    state_out.start()
    mamba_y = (y_v[...] + ref["sg"][...] * active) * gate

    def share(used, weight, square, send, recv, k):
        proj = dot(used, weight)
        extra = jnp.zeros((ROWS, 13 * LANES - proj.shape[1]), F32)
        proj = jnp.concatenate([proj, extra], axis=1)
        tail = iota((ROWS, TP_PAD), 1) >= TP_COLS
        for p in range(tp_n):
            moved = proj if p == 0 else pltpu.roll(proj, proj.shape[1] - p * TP_COLS, 1)
            send[p] = jnp.where(tail, square, moved[:, 0:TP_PAD])
        recv[tp] = send[tp]
        tp_start(lambda p: send.at[p], recv, k)

    def gathered(recv, k):
        wait_all(recv, k, tp_n - 1, "recv")
        total = recv[0]
        for p in range(1, tp_n):
            total = total + recv[p]
        return total

    mamba_square = jnp.sum(mamba_y * mamba_y, axis=1, keepdims=True)
    share((mamba_y * ref["mg"][...]).astype(BF16), ref["mo"][...], mamba_square, m_send, m_recv, 2)

    o_slot[...] = jnp.zeros_like(o_slot)
    q_slot[...] = jnp.zeros_like(q_slot)
    wait_all(q_all, 0, n - 1, "recv")
    q_sel = dot(own_pick, q_all[...].reshape(n * 8, 3 * LANES))
    low40 = iota((SPAD, LANES), 1) < HD
    for h in range(HEADS):
        col = q_sel[:, (h // 2) * LANES : (h // 2 + 1) * LANES]
        if h % 2 == 1:
            col = pltpu.roll(col, HD, 1)
        q_slot[h * SPAD : (h + 1) * SPAD, :] = jnp.where(low40, col, 0.0) * HD**-0.5
    copies["cache"].wait()
    block = ref["cache"].shape[1]
    time = iota((16, block), 1)
    first = iota((16, block), 0) < 8

    def live(s):
        owner = ref["sr_s"][s]
        used = owner >= 0
        return jnp.where(used, ref["len_s"][jnp.where(used, owner, 0)] - ref["sb_s"][s] * block, 0)

    def attend(p, carry):
        s0 = 2 * p
        s1 = s0 + 1
        pair = jnp.concatenate([ref["cache"][s0], ref["cache"][s1]], axis=1)
        q0 = q_slot[pl.ds(s0, 8, stride=SPAD), :]
        q1 = q_slot[pl.ds(s1, 8, stride=SPAD), :]
        zero = jnp.zeros_like(q0)
        lhs = jnp.concatenate(
            [jnp.concatenate([q0, zero], axis=1), jnp.concatenate([zero, q1], axis=1)], axis=0
        ).astype(BF16)
        scores = dot_nt(lhs, pair)
        ok = time < jnp.where(first, live(s0), live(s1))
        scores = jnp.where(ok, scores, NEG)
        top = jnp.max(scores, axis=1, keepdims=True)
        weights = jnp.where(ok, jnp.exp(scores - top), 0.0).astype(BF16)
        total = jnp.sum(weights.astype(F32), axis=1, keepdims=True)
        total = jnp.where(total > 0.0, total, 1.0)
        out = dot(weights, pair)
        lse = top + jnp.log(total)
        inv = 1.0 / total
        o_slot[pl.ds(s0, 8, stride=SPAD), :] = jnp.where(low8, lse[0:8], out[0:8, 0:LANES] * inv[0:8])
        o_slot[pl.ds(s1, 8, stride=SPAD), :] = jnp.where(low8, lse[8:16], out[8:16, LANES:] * inv[8:16])
        return carry

    lax.fori_loop(0, slots // 2, attend, 0)

    lane40v = iota((SPAD, LANES), 1)
    outs = [o_slot[h * SPAD : (h + 1) * SPAD, :] for h in range(HEADS)]
    turned = [pltpu.roll(o, HD, 1) for o in outs]
    tail = jnp.where(lane40v == 80, ((sr_col & 7) + 1).astype(F32), 0.0)
    for h in range(HEADS):
        rest = turned[h]
        for t in range(3):
            term = rest.astype(BF16).astype(F32)
            tail = jnp.where(lane40v == HD + 3 * h + t, term, tail)
            rest = rest - term
    table = jnp.concatenate(
        [
            jnp.where(low40, turned[0], outs[1]),
            jnp.where(low40, turned[2], outs[3]),
            jnp.where(low40, turned[4], tail),
            jnp.zeros((8, LANES), F32),
        ],
        axis=0,
    ).astype(BF16)
    msg[...] = dot(pick, table).reshape(n, 8, LANES).astype(BF16)
    inbox[me] = msg[me]

    def deliver(i, carry):
        d = lax.rem(me + i, n)
        pltpu.make_async_remote_copy(
            src_ref=msg.at[d], dst_ref=inbox.at[me], send_sem=send_sem.at[3], recv_sem=recv_sem.at[3],
            device_id={"req": d},
        ).start()
        return carry

    lax.fori_loop(1, n, deliver, 0)

    mamba = gathered(m_recv, 2)
    mamba_scale = jnp.sqrt(mamba[:, TP_COLS : TP_COLS + 1] * (1.0 / (TP_COLS * tp_n)) + 1e-06)
    wide = jnp.concatenate([hidden, jnp.zeros((ROWS, 13 * LANES - width), F32)], axis=1)
    residual = wide[:, 0:TP_PAD]
    for p in range(1, tp_n):
        residual = jnp.where(tp == p, pltpu.roll(wide, wide.shape[1] - p * TP_COLS, 1)[:, 0:TP_PAD], residual)
    base = residual + 0.5 * (mamba / mamba_scale)
    e_row = iota((16, LANES), 0)
    e_lane = iota((16, LANES), 1)
    e_start = HD + 3 * e_row
    spread_rows = ((e_row < HEADS) & (e_lane >= e_start) & (e_lane < e_start + 3)) | ((e_row == HEADS) & (e_lane == 80))
    spread_rows = jnp.where(spread_rows, 1.0, 0.0).astype(BF16)
    copies["ag"].wait()
    copies["wo"].wait()

    wait_all(inbox, 3, n - 1, "recv")
    box = inbox[...].reshape(n * 8, LANES)
    heads_row = dot_nt(spread_rows, box)
    col_j = lax.shift_right_arithmetic(iota((ROWS, n * 8), 1) & 7, 1)
    r_id = (iota((ROWS, n * 8), 0) + 1).astype(F32)
    shifted = [pltpu.roll(heads_row, n * 8 - (4 - 2 * j), 1) if j < 2 else heads_row for j in range(3)]
    high, low, den, own_w = [], [], [], []
    for h in range(HEADS):
        j = h // 2
        lse = jnp.broadcast_to(shifted[j][h : h + 1, :], (ROWS, n * 8))
        rid = jnp.broadcast_to(shifted[j][HEADS : HEADS + 1, :], (ROWS, n * 8))
        mine = (rid == r_id) & (col_j == j)
        top = jnp.maximum(jnp.max(jnp.where(mine, lse, NEG), axis=1, keepdims=True), own_score[h])
        w = jnp.where(mine, jnp.exp(lse - top), 0.0)
        own = jnp.exp(own_score[h] - top)
        den.append(jnp.sum(w, axis=1, keepdims=True) + own)
        own_w.append(own)
        w_high = w.astype(BF16).astype(F32)
        high.append(w_high)
        low.append(w - w_high)
    merged = dot(jnp.concatenate(high + low, axis=0).astype(BF16), box)
    numer = [
        merged[h * 8 : h * 8 + 8] + merged[(HEADS + h) * 8 : (HEADS + h) * 8 + 8] + own_w[h] * value_both
        for h in range(HEADS)
    ]
    normal = [numer[h] / den[h] for h in range(HEADS)]
    attention = jnp.concatenate(
        [
            jnp.where(low8, normal[0], normal[1]),
            jnp.where(low8, normal[2], normal[3]),
            jnp.where(low8, normal[4], 0.0),
        ],
        axis=1,
    )[:, 0 : HEADS * HD]
    attn_square = jnp.sum(attention * attention, axis=1, keepdims=True)
    share((attention * ref["ag"][...]).astype(BF16), ref["wo"][...], attn_square, a_send, a_recv, 4)
    attn = gathered(a_recv, 4)
    attn_scale = jnp.sqrt(attn[:, TP_COLS : TP_COLS + 1] * (1.0 / (HEADS * HD * tp_n)) + 1e-06)
    final = base + 0.5 * (attn / attn_scale)
    layer_v[...] = final[:, 0:TP_COLS].astype(BF16)
    layer_out = pltpu.make_async_copy(layer_v, out_layer, out_sem.at[1])
    layer_out.start()
    wait_all(q_all, 0, n - 1, "send")
    wait_all(sel_buf, 1, tp_n - 1, "send")
    wait_all(m_send, 2, tp_n - 1, "send")
    wait_all(msg, 3, n - 1, "send")
    wait_all(a_send, 4, tp_n - 1, "send")
    state_out.wait()
    layer_out.wait()


def body(
    hidden_in, norm_gain, query_weight, memory_weight, attention_out, attention_gain, mamba_input, conv_weight,
    conv_state, select_weight, step_weight, step_bias, decay_log, skip_gain, scan_state, mamba_gain, mamba_out,
    cache_blocks, lengths, slot_request, slot_block,
):
    n = lax.axis_size("req")
    tp_n = lax.axis_size("tp")
    slots, _, block, kv = cache_blocks.shape
    rate = 10000.0 ** (-(np.arange(LANES) % (HD // 2)) * (2.0 / HD))
    freq = jnp.asarray(np.broadcast_to(rate[None, :], (ROWS, LANES)), F32)
    row = lambda v: v.reshape(1, -1)
    operand = {
        "len_s": lengths,
        "sr_s": slot_request,
        "sb_s": slot_block,
        "hidden": hidden_in,
        "gain": row(norm_gain),
        "freq": freq,
        "wq": query_weight.T,
        "wm": memory_weight,
        "mi": jnp.transpose(mamba_input, (0, 2, 1)),
        "cw": conv_weight,
        "cs": jnp.transpose(conv_state, (1, 0, 2)),
        "sw": select_weight.T,
        "st": step_weight.T,
        "sb": row(step_bias),
        "dl": decay_log,
        "sg": row(skip_gain),
        "ss": scan_state,
        "mg": row(mamba_gain),
        "mo": mamba_out,
        "cache": cache_blocks.reshape(slots, block, kv),
        "ag": row(attention_gain),
        "wo": attention_out,
    }
    operand = [operand[name] for name in LOCAL]
    scratch = []
    for name, v in zip(LOCAL, operand):
        space = pltpu.SMEM if name in ("len_s", "sr_s", "sb_s") else pltpu.VMEM
        shape = (v.shape[0] + 64, v.shape[1]) if name == "wq" else v.shape
        scratch.append(space(shape, v.dtype))
    scratch += [
        pltpu.VMEM((n, ROWS, 3 * LANES), BF16),
        pltpu.VMEM((tp_n, ROWS, 2 * LANES), F32),
        pltpu.VMEM((n, 8, LANES), BF16),
        pltpu.VMEM((n, 8, LANES), BF16),
        pltpu.VMEM((tp_n, ROWS, TP_PAD), F32),
        pltpu.VMEM((tp_n, ROWS, TP_PAD), F32),
        pltpu.VMEM((tp_n, ROWS, TP_PAD), F32),
        pltpu.VMEM((tp_n, ROWS, TP_PAD), F32),
        pltpu.VMEM((8 * SPAD, LANES), F32),
        pltpu.VMEM((8 * SPAD, LANES), F32),
        pltpu.VMEM(scan_state.shape, F32),
        pltpu.VMEM((ROWS, TP_COLS), BF16),
        pltpu.VMEM((ROWS, TP_COLS), F32),
        pltpu.SemaphoreType.DMA((len(LOCAL),)),
        pltpu.SemaphoreType.DMA((2,)),
        pltpu.SemaphoreType.DMA((5,)),
        pltpu.SemaphoreType.DMA((5,)),
    ]

    def step(*refs):
        kernel(n, tp_n, slots, *refs)

    return pl.pallas_call(
        step,
        out_shape=(
            jax.ShapeDtypeStruct((ROWS, TP_COLS), BF16),
            jax.ShapeDtypeStruct(scan_state.shape, F32),
        ),
        in_specs=[pl.BlockSpec(memory_space=pl.ANY)] * len(operand),
        out_specs=(pl.BlockSpec(memory_space=pl.ANY),) * 2,
        scratch_shapes=scratch,
        compiler_params=pltpu.CompilerParams(collective_id=0, has_side_effects=True),
        name="decode_layer",
    )(*operand)


def solution(mesh):
    return jax.shard_map(
        body,
        mesh=mesh,
        in_specs=(
            P("req", None),
            P(),
            P(None, "tp"),
            P(None, "tp"),
            P("tp", None),
            P("tp"),
            P(None, None, "tp"),
            P(None, "tp"),
            P("req", None, "tp"),
            P("tp", None),
            P(None, "tp"),
            P("tp"),
            P(None, "tp"),
            P("tp"),
            P("req", None, "tp"),
            P("tp"),
            P("tp", None),
            P("req", "tp", None, None),
            P(),
            P("req"),
            P("req"),
        ),
        out_specs=(P("req", "tp"), P("req", None, "tp")),
        check_vma=False,
    )
```

```python
import math

import jax
import jax.numpy as jnp
import numpy as np
from jax import lax
from jax.experimental import pallas as pl
from jax.experimental.pallas import tpu as pltpu
from jax.sharding import PartitionSpec as P

F32 = jnp.float32
BF16 = jnp.bfloat16
NEG = -1e30
ROWS = 8
HEADS = 5
HD = 64
LANES = 128
SPAD = 40
TP_COLS = 400
TP_PAD = 512
NT = (((1,), (1,)), ((), ()))


def depth_of(n):
    return 8 if n >= 32 else n // 4


def iota(shape, axis):
    return lax.broadcasted_iota(jnp.int32, shape, axis)


def dot(a, b):
    return jnp.dot(a, b, preferred_element_type=F32)


def dot_nt(a, b):
    return lax.dot_general(a, b, NT, preferred_element_type=F32)


def silu(v):
    return v * (1.0 / (1.0 + jnp.exp(-v)))


def softplus(v):
    return jnp.maximum(v, 0.0) + jnp.log1p(jnp.exp(-jnp.abs(v)))


LOCAL = (
    "len_s", "sr_s", "sb_s", "hidden", "gain", "freq", "wq", "wm", "mi", "cw", "cs", "sw", "st", "sb", "dl", "sg",
    "ss", "mg", "mo", "cache", "ag", "wo",
)


def kernel(n, tp_n, slots, *refs):
    hbm = dict(zip(LOCAL, refs[: len(LOCAL)]))
    out_layer, out_state = refs[len(LOCAL) : len(LOCAL) + 2]
    refs = refs[len(LOCAL) + 2 :]
    ref = dict(zip(LOCAL, refs[: len(LOCAL)]))
    (
        q_all, sel_buf, msg, inbox, m_send, m_recv, a_send, a_recv, q_slot, o_slot, y_v,
        in_sem, send_sem, recv_sem, z_sem,
    ) = refs[len(LOCAL) :]
    me = lax.axis_index("req")
    tp = lax.axis_index("tp")

    z_n = depth_of(n)
    plane_n = n // z_n
    core = lax.rem(me, 2)
    z = lax.rem(me // 2, z_n)
    place = me // (2 * z_n) * 2 + core

    def at(place, z):
        return place // 2 * (2 * z_n) + z * 2 + lax.rem(place, 2)

    z_order = sorted(range(1, z_n), key=lambda i: (min(i, z_n - i), i))
    column = {i: at(place, lax.rem(z + i, z_n)) for i in z_order}
    plane = [at(lax.rem(place + j, plane_n), z) for j in range(1, plane_n)]

    copies = {}
    for k, name in enumerate(LOCAL):
        dst = ref[name].at[pl.ds(0, HEADS * HD)] if name == "wq" else ref[name]
        copies[name] = pltpu.make_async_copy(hbm[name], dst, in_sem.at[k])
        copies[name].start()

    barrier = pltpu.get_barrier_semaphore()
    for i in reversed(z_order):
        pl.semaphore_signal(barrier, inc=1, device_id={"req": column[i]})
    for d in plane:
        pl.semaphore_signal(barrier, inc=1, device_id={"req": d})
    for i in range(1, tp_n):
        pl.semaphore_signal(barrier, inc=1, device_id={"tp": lax.rem(tp + i, tp_n)})
    inbox[...] = jnp.zeros_like(inbox)

    def tp_start(src, dst, k):
        for i in range(1, tp_n):
            p = lax.rem(tp + i, tp_n)
            pltpu.make_async_remote_copy(
                src_ref=src(p), dst_ref=dst.at[tp], send_sem=send_sem.at[k], recv_sem=recv_sem.at[k],
                device_id={"tp": p},
            ).start()

    def wait_all(buf, k, count, which):
        view = buf.at[pl.ds(0, count), pl.ds(0, 6)] if k == 3 else buf.at[pl.ds(0, count)]
        copy = pltpu.make_async_remote_copy(
            src_ref=view, dst_ref=view, send_sem=send_sem.at[k], recv_sem=recv_sem.at[k], device_id={"tp": tp}
        )
        if which == "send":
            copy.wait_send()
        else:
            copy.wait_recv()

    lane8 = iota((ROWS, LANES), 1)
    low8 = lane8 < HD

    ref["wq"][pl.ds(HEADS * HD, 64), :] = jnp.zeros((64, ref["wq"].shape[1]), BF16)
    copies["hidden"].wait()
    copies["gain"].wait()
    hidden = ref["hidden"][...].astype(F32)
    width = hidden.shape[1]
    mean = jnp.sum(hidden * hidden, axis=1, keepdims=True) * (1.0 / width)
    normed = (hidden * lax.rsqrt(mean + 1e-06) * ref["gain"][...].reshape(1, width)).astype(BF16)

    for name in ("len_s", "sr_s", "sb_s", "freq"):
        copies[name].wait()
    position = jnp.zeros((ROWS, LANES), F32)
    row8 = iota((ROWS, LANES), 0)
    for r in range(ROWS):
        position = jnp.where(row8 == r, ref["len_s"][me * ROWS + r].astype(F32), position)
    angles = position * ref["freq"][...]
    cosine = jnp.cos(angles)
    sine = jnp.sin(angles)
    front = (lane8 & (HD - 1)) < HD // 2

    def rot(v):
        other = jnp.where(front, -pltpu.roll(v, LANES - HD // 2, 1), pltpu.roll(v, HD // 2, 1))
        return v * cosine + other * sine

    copies["wq"].wait()
    q_raw = dot_nt(normed, ref["wq"][...])
    query = [rot(q_raw[:, c * LANES : (c + 1) * LANES]).astype(BF16) for c in range(3)]
    for c in range(3):
        q_all[me, :, c * LANES : (c + 1) * LANES] = query[c]

    pl.semaphore_wait(barrier, len(z_order) + len(plane) + tp_n - 1)

    def z_copy(i, source, target):
        return pltpu.make_async_remote_copy(
            src_ref=q_all.at[source], dst_ref=q_all.at[source], send_sem=send_sem.at[0], recv_sem=z_sem.at[i - 1],
            device_id={"req": target},
        )

    def pass_on(source):
        for d in plane:
            pltpu.make_async_remote_copy(
                src_ref=q_all.at[source], dst_ref=q_all.at[source], send_sem=send_sem.at[0], recv_sem=recv_sem.at[0],
                device_id={"req": d},
            ).start()

    def pass_on_from(distance):
        for i in z_order:
            if min(i, z_n - i) == distance:
                source = at(place, lax.rem(z + z_n - i, z_n))
                z_copy(i, source, source).wait_recv()
                pass_on(source)

    for i in reversed(z_order):
        z_copy(i, me, column[i]).start()
    pass_on(me)

    copies["mi"].wait()
    mamba_x = dot_nt(normed, ref["mi"][0]).astype(BF16)
    for name in ("cw", "cs", "sw"):
        copies[name].wait()
    taps = ref["cw"].shape[0]
    conv = ref["cw"][taps - 1 : taps, :] * mamba_x.astype(F32)
    for j in range(taps - 1):
        conv = conv + ref["cw"][j : j + 1, :] * ref["cs"][j].astype(F32)
    activated = silu(conv).astype(BF16)
    part = dot_nt(activated, ref["sw"][...])
    sel_buf[tp] = jnp.concatenate([part, jnp.zeros((ROWS, 2 * LANES - part.shape[1]), F32)], axis=1)
    tp_start(lambda p: sel_buf.at[tp], sel_buf, 1)

    pass_on_from(1)
    gate = silu(dot_nt(normed, ref["mi"][1]))
    pass_on_from(2)
    copies["wm"].wait()
    memory = dot(normed, ref["wm"][...])
    key_value = jnp.where(low8, rot(memory), memory).astype(BF16).astype(F32)
    swapped = pltpu.roll(key_value, HD, 1)
    key_both = jnp.where(low8, key_value, swapped)
    value_both = jnp.where(low8, swapped, key_value)

    own_score = []
    for h in range(HEADS):
        half = low8 if h % 2 == 0 else jnp.logical_not(low8)
        prod = jnp.where(half, query[h // 2].astype(F32) * key_both, 0.0)
        own_score.append(jnp.sum(prod, axis=1, keepdims=True) * HD**-0.5)

    pass_on_from(3)
    lane40 = lax.rem(lane8, SPAD)
    lane40 = jnp.where(lane8 < 3 * SPAD, lane40, -1)
    sr_row = jnp.full((ROWS, LANES), -1, jnp.int32)
    sub_col = iota((SPAD, LANES), 0)
    sr_col = jnp.full((SPAD, LANES), -1, jnp.int32)
    for s in range(slots):
        v = ref["sr_s"][s]
        sr_row = jnp.where(lane40 == s, v, sr_row)
        sr_col = jnp.where(sub_col == s, v, sr_col)
    dest_row = lax.shift_right_arithmetic(sr_row, 3)
    rank_row = jnp.zeros((ROWS, LANES), jnp.int32)
    for s in range(slots):
        d = lax.shift_right_arithmetic(ref["sr_s"][s], 3)
        rank_row = rank_row + jnp.where((dest_row == d) & (lane40 > s), 1, 0)
    m_rows = n * 8
    mr = iota((m_rows, LANES), 0)
    mj = lax.shift_right_arithmetic(mr & 7, 1)
    cj = jnp.where(lane8 < SPAD, 0, jnp.where(lane8 < 2 * SPAD, 1, jnp.where(lane8 < 3 * SPAD, 2, -1)))
    pick = (
        (lax.shift_right_arithmetic(mr, 3) == dest_row[0:1, :])
        & ((mr & 1) == rank_row[0:1, :])
        & (mj == cj[0:1, :])
    )
    pick = jnp.where(pick, 1.0, 0.0).astype(BF16)
    own_pick = jnp.concatenate([sr_col] * (n * 8 // LANES), axis=1) if n * 8 >= LANES else sr_col[:, 0 : n * 8]
    own_pick = jnp.where(own_pick == iota((SPAD, n * 8), 1), 1.0, 0.0).astype(BF16)

    for distance in range(4, z_n // 2 + 1):
        pass_on_from(distance)
    wait_all(sel_buf, 1, tp_n - 1, "recv")
    selection = sel_buf[0]
    for p in range(1, tp_n):
        selection = selection + sel_buf[p]
    dtr = ref["st"].shape[1]
    ns = ref["dl"].shape[0]
    for name in ("st", "sb", "dl", "sg", "ss", "mg", "mo"):
        copies[name].wait()
    step = softplus(dot_nt(selection[:, 0:dtr].astype(BF16), ref["st"][...]) + ref["sb"][...])
    maps = pltpu.roll(selection, selection.shape[1] - dtr, 1)[:, 0:LANES]
    maps = jnp.transpose(maps)
    active = activated.astype(F32)
    decay = jnp.exp(ref["dl"][...])
    drive = step * active
    for r in range(ROWS):
        new = (
            jnp.exp(-step[r : r + 1, :] * decay) * ref["ss"][r]
            + drive[r : r + 1, :] * maps[0:ns, r : r + 1]
        )
        out_state[r] = new
        y_v[r : r + 1, :] = jnp.sum(maps[ns : 2 * ns, r : r + 1] * new, axis=0, keepdims=True)
    mamba_y = (y_v[...] + ref["sg"][...] * active) * gate

    def share(used, weight, square, send, recv, k):
        proj = dot(used, weight)
        extra = jnp.zeros((ROWS, 13 * LANES - proj.shape[1]), F32)
        proj = jnp.concatenate([proj, extra], axis=1)
        tail = iota((ROWS, TP_PAD), 1) >= TP_COLS
        for p in range(tp_n):
            moved = proj if p == 0 else pltpu.roll(proj, proj.shape[1] - p * TP_COLS, 1)
            send[p] = jnp.where(tail, square, moved[:, 0:TP_PAD])
        recv[tp] = send[tp]
        tp_start(lambda p: send.at[p], recv, k)

    def gathered(recv, k):
        wait_all(recv, k, tp_n - 1, "recv")
        total = recv[0]
        for p in range(1, tp_n):
            total = total + recv[p]
        return total

    mamba_square = jnp.sum(mamba_y * mamba_y, axis=1, keepdims=True)
    share((mamba_y * ref["mg"][...]).astype(BF16), ref["mo"][...], mamba_square, m_send, m_recv, 2)

    o_slot[...] = jnp.zeros_like(o_slot)
    q_slot[...] = jnp.zeros_like(q_slot)
    wait_all(q_all, 0, n - z_n, "recv")
    q_sel = dot(own_pick, q_all[...].reshape(n * 8, 3 * LANES))
    low40 = iota((SPAD, LANES), 1) < HD
    for h in range(HEADS):
        col = q_sel[:, (h // 2) * LANES : (h // 2 + 1) * LANES]
        if h % 2 == 1:
            col = pltpu.roll(col, HD, 1)
        q_slot[h * SPAD : (h + 1) * SPAD, :] = jnp.where(low40, col, 0.0) * HD**-0.5
    copies["cache"].wait()
    block = ref["cache"].shape[1]
    time = iota((16, block), 1)
    first = iota((16, block), 0) < 8

    def live(s):
        owner = ref["sr_s"][s]
        used = owner >= 0
        return jnp.where(used, ref["len_s"][jnp.where(used, owner, 0)] - ref["sb_s"][s] * block, 0)

    def attend(p, carry):
        s0 = 2 * p
        s1 = s0 + 1
        pair = jnp.concatenate([ref["cache"][s0], ref["cache"][s1]], axis=1)
        q0 = q_slot[pl.ds(s0, 8, stride=SPAD), :]
        q1 = q_slot[pl.ds(s1, 8, stride=SPAD), :]
        zero = jnp.zeros_like(q0)
        lhs = jnp.concatenate(
            [jnp.concatenate([q0, zero], axis=1), jnp.concatenate([zero, q1], axis=1)], axis=0
        ).astype(BF16)
        scores = dot_nt(lhs, pair)
        ok = time < jnp.where(first, live(s0), live(s1))
        scores = jnp.where(ok, scores, NEG)
        top = jnp.max(scores, axis=1, keepdims=True)
        weights = jnp.where(ok, jnp.exp(scores - top), 0.0).astype(BF16)
        total = jnp.sum(weights.astype(F32), axis=1, keepdims=True)
        total = jnp.where(total > 0.0, total, 1.0)
        out = dot(weights, pair)
        lse = top + jnp.log(total)
        inv = 1.0 / total
        o_slot[pl.ds(s0, 8, stride=SPAD), :] = jnp.where(low8, lse[0:8], out[0:8, 0:LANES] * inv[0:8])
        o_slot[pl.ds(s1, 8, stride=SPAD), :] = jnp.where(low8, lse[8:16], out[8:16, LANES:] * inv[8:16])
        return carry

    lax.fori_loop(0, slots // 2, attend, 0, unroll=True)

    lane40v = iota((SPAD, LANES), 1)
    outs = [o_slot[h * SPAD : (h + 1) * SPAD, :] for h in range(HEADS)]
    turned = [pltpu.roll(o, HD, 1) for o in outs]
    tail = jnp.where(lane40v == 80, ((sr_col & 7) + 1).astype(F32), 0.0)
    for h in range(HEADS):
        rest = turned[h]
        for t in range(3):
            term = rest.astype(BF16).astype(F32)
            tail = jnp.where(lane40v == HD + 3 * h + t, term, tail)
            rest = rest - term
    table = jnp.concatenate(
        [
            jnp.where(low40, turned[0], outs[1]),
            jnp.where(low40, turned[2], outs[3]),
            jnp.where(low40, turned[4], tail),
            jnp.zeros((8, LANES), F32),
        ],
        axis=0,
    ).astype(BF16)
    msg[...] = dot(pick, table).reshape(n, 8, LANES).astype(BF16)
    inbox[me] = msg[me]

    def deliver(i, carry):
        d = lax.rem(me + i, n)
        pltpu.make_async_remote_copy(
            src_ref=msg.at[d, pl.ds(0, 6)], dst_ref=inbox.at[me, pl.ds(0, 6)], send_sem=send_sem.at[3], recv_sem=recv_sem.at[3],
            device_id={"req": d},
        ).start()
        return carry

    lax.fori_loop(1, n, deliver, 0, unroll=7)

    mamba = gathered(m_recv, 2)
    mamba_scale = jnp.sqrt(mamba[:, TP_COLS : TP_COLS + 1] * (1.0 / (TP_COLS * tp_n)) + 1e-06)
    wide = jnp.concatenate([hidden, jnp.zeros((ROWS, 13 * LANES - width), F32)], axis=1)
    residual = wide[:, 0:TP_PAD]
    for p in range(1, tp_n):
        residual = jnp.where(tp == p, pltpu.roll(wide, wide.shape[1] - p * TP_COLS, 1)[:, 0:TP_PAD], residual)
    base = residual + 0.5 * (mamba / mamba_scale)
    e_row = iota((16, LANES), 0)
    e_lane = iota((16, LANES), 1)
    e_start = HD + 3 * e_row
    spread_rows = ((e_row < HEADS) & (e_lane >= e_start) & (e_lane < e_start + 3)) | ((e_row == HEADS) & (e_lane == 80))
    spread_rows = jnp.where(spread_rows, 1.0, 0.0).astype(BF16)
    copies["ag"].wait()
    copies["wo"].wait()

    wait_all(inbox, 3, n - 1, "recv")
    box = inbox[...].reshape(n * 8, LANES)
    heads_row = dot_nt(spread_rows, box)
    col_j = lax.shift_right_arithmetic(iota((ROWS, n * 8), 1) & 7, 1)
    r_id = (iota((ROWS, n * 8), 0) + 1).astype(F32)
    shifted = [pltpu.roll(heads_row, n * 8 - (4 - 2 * j), 1) if j < 2 else heads_row for j in range(3)]
    high, low, den, own_w = [], [], [], []
    for h in range(HEADS):
        j = h // 2
        lse = jnp.broadcast_to(shifted[j][h : h + 1, :], (ROWS, n * 8))
        rid = jnp.broadcast_to(shifted[j][HEADS : HEADS + 1, :], (ROWS, n * 8))
        mine = (rid == r_id) & (col_j == j)
        top = jnp.maximum(jnp.max(jnp.where(mine, lse, NEG), axis=1, keepdims=True), own_score[h])
        w = jnp.where(mine, jnp.exp(lse - top), 0.0)
        own = jnp.exp(own_score[h] - top)
        den.append(jnp.sum(w, axis=1, keepdims=True) + own)
        own_w.append(own)
        w_high = w.astype(BF16).astype(F32)
        high.append(w_high)
        low.append(w - w_high)
    merged = dot(jnp.concatenate(high + low, axis=0).astype(BF16), box)
    numer = [
        merged[h * 8 : h * 8 + 8] + merged[(HEADS + h) * 8 : (HEADS + h) * 8 + 8] + own_w[h] * value_both
        for h in range(HEADS)
    ]
    normal = [numer[h] / den[h] for h in range(HEADS)]
    attention = jnp.concatenate(
        [
            jnp.where(low8, normal[0], normal[1]),
            jnp.where(low8, normal[2], normal[3]),
            jnp.where(low8, normal[4], 0.0),
        ],
        axis=1,
    )[:, 0 : HEADS * HD]
    attn_square = jnp.sum(attention * attention, axis=1, keepdims=True)
    share((attention * ref["ag"][...].reshape(1, HEADS * HD)).astype(BF16), ref["wo"][...], attn_square, a_send, a_recv, 4)
    attn = gathered(a_recv, 4)
    attn_scale = jnp.sqrt(attn[:, TP_COLS : TP_COLS + 1] * (1.0 / (HEADS * HD * tp_n)) + 1e-06)
    final = base + 0.5 * (attn / attn_scale)
    out_layer[...] = final[:, 0:TP_COLS].astype(BF16)
    wait_all(q_all, 0, n - 1, "send")
    wait_all(sel_buf, 1, tp_n - 1, "send")
    wait_all(m_send, 2, tp_n - 1, "send")
    wait_all(msg, 3, n - 1, "send")
    wait_all(a_send, 4, tp_n - 1, "send")


def write_out(layer, state, layer_out, state_out, sem):
    first = pltpu.make_async_copy(state, state_out, sem.at[0])
    second = pltpu.make_async_copy(layer, layer_out, sem.at[1])
    first.start()
    second.start()
    first.wait()
    second.wait()


def body(
    hidden_in, norm_gain, query_weight, memory_weight, attention_out, attention_gain, mamba_input, conv_weight,
    conv_state, select_weight, step_weight, step_bias, decay_log, skip_gain, scan_state, mamba_gain, mamba_out,
    cache_blocks, lengths, slot_request, slot_block,
):
    n = lax.axis_size("req")
    tp_n = lax.axis_size("tp")
    slots, _, block, kv = cache_blocks.shape
    rate = 10000.0 ** (-(np.arange(LANES) % (HD // 2)) * (2.0 / HD))
    freq = jnp.asarray(np.broadcast_to(rate[None, :], (ROWS, LANES)), F32)
    row = lambda v: v.reshape(1, -1)
    operand = {
        "len_s": lengths,
        "sr_s": slot_request,
        "sb_s": slot_block,
        "hidden": hidden_in,
        "gain": norm_gain,
        "freq": freq,
        "wq": query_weight.T,
        "wm": memory_weight,
        "mi": jnp.transpose(mamba_input, (0, 2, 1)),
        "cw": conv_weight,
        "cs": jnp.transpose(conv_state, (1, 0, 2)),
        "sw": select_weight.T,
        "st": step_weight.T,
        "sb": row(step_bias),
        "dl": decay_log,
        "sg": row(skip_gain),
        "ss": scan_state,
        "mg": row(mamba_gain),
        "mo": mamba_out,
        "cache": cache_blocks.reshape(slots, block, kv),
        "ag": attention_gain,
        "wo": attention_out,
    }
    operand = [pltpu.with_memory_space_constraint(operand[name], pltpu.HBM) for name in LOCAL]
    scratch = []
    for name, v in zip(LOCAL, operand):
        space = pltpu.SMEM if name in ("len_s", "sr_s", "sb_s") else pltpu.VMEM
        shape = (v.shape[0] + 64, v.shape[1]) if name == "wq" else v.shape
        scratch.append(space(shape, v.dtype))
    scratch += [
        pltpu.VMEM((n, ROWS, 3 * LANES), BF16),
        pltpu.VMEM((tp_n, ROWS, 2 * LANES), F32),
        pltpu.VMEM((n, 8, LANES), BF16),
        pltpu.VMEM((n, 8, LANES), BF16),
        pltpu.VMEM((tp_n, ROWS, TP_PAD), F32),
        pltpu.VMEM((tp_n, ROWS, TP_PAD), F32),
        pltpu.VMEM((tp_n, ROWS, TP_PAD), F32),
        pltpu.VMEM((tp_n, ROWS, TP_PAD), F32),
        pltpu.VMEM((8 * SPAD, LANES), F32),
        pltpu.VMEM((8 * SPAD, LANES), F32),
        pltpu.VMEM((ROWS, TP_COLS), F32),
        pltpu.SemaphoreType.DMA((len(LOCAL),)),
        pltpu.SemaphoreType.DMA((5,)),
        pltpu.SemaphoreType.DMA((5,)),
        pltpu.SemaphoreType.DMA((max(1, depth_of(n) - 1),)),
    ]

    def step(*refs):
        kernel(n, tp_n, slots, *refs)

    layer, state = pl.pallas_call(
        step,
        out_shape=(
            jax.ShapeDtypeStruct((ROWS, TP_COLS), BF16),
            jax.ShapeDtypeStruct(scan_state.shape, F32),
        ),
        in_specs=[pl.BlockSpec(memory_space=pltpu.HBM)] * len(operand),
        out_specs=(pl.BlockSpec(memory_space=pltpu.VMEM),) * 2,
        scratch_shapes=scratch,
        compiler_params=pltpu.CompilerParams(collective_id=0, has_side_effects=True, vmem_limit_bytes=24 << 20),
        name="decode_layer",
    )(*operand)
    results = (jax.ShapeDtypeStruct(layer.shape, BF16), jax.ShapeDtypeStruct(state.shape, F32))
    return pl.pallas_call(
        write_out,
        out_shape=results,
        in_specs=[pl.BlockSpec(memory_space=pltpu.VMEM)] * 2,
        out_specs=(pl.BlockSpec(memory_space=pl.ANY),) * 2,
        scratch_shapes=[pltpu.SemaphoreType.DMA((2,))],
        compiler_params=pltpu.CompilerParams(vmem_limit_bytes=1 << 20),
        name="write_out",
    )(layer, state)


def solution(mesh):
    return jax.shard_map(
        body,
        mesh=mesh,
        in_specs=(
            P("req", None),
            P(),
            P(None, "tp"),
            P(None, "tp"),
            P("tp", None),
            P("tp"),
            P(None, None, "tp"),
            P(None, "tp"),
            P("req", None, "tp"),
            P("tp", None),
            P(None, "tp"),
            P("tp"),
            P(None, "tp"),
            P("tp"),
            P("req", None, "tp"),
            P("tp"),
            P("tp", None),
            P("req", "tp", None, None),
            P(),
            P("req"),
            P("req"),
        ),
        out_specs=(P("req", "tp"), P("req", None, "tp")),
        check_vma=False,
    )
```

```python
import math

import jax
import jax.numpy as jnp
import numpy as np
from jax import lax
from jax.experimental import pallas as pl
from jax.experimental.pallas import tpu as pltpu
from jax.sharding import PartitionSpec as P

F32 = jnp.float32
BF16 = jnp.bfloat16
NEG = -1e30
ROWS = 8
HEADS = 5
HD = 64
LANES = 128
SPAD = 40
TP_COLS = 400
TP_PAD = 512
NT = (((1,), (1,)), ((), ()))


def depth_of(n):
    return 8 if n >= 32 else n // 4


def iota(shape, axis):
    return lax.broadcasted_iota(jnp.int32, shape, axis)


def dot(a, b):
    return jnp.dot(a, b, preferred_element_type=F32)


def dot_nt(a, b):
    return lax.dot_general(a, b, NT, preferred_element_type=F32)


def silu(v):
    return v * (1.0 / (1.0 + jnp.exp(-v)))


def softplus(v):
    return jnp.maximum(v, 0.0) + jnp.log1p(jnp.exp(-jnp.abs(v)))


LOCAL = (
    "len_s", "sr_s", "sb_s", "hidden", "gain", "freq", "wq", "wm", "mi", "cw", "cs", "sw", "st", "sb", "dl", "sg",
    "ss", "mg", "mo", "cache", "ag", "wo",
)


def kernel(n, tp_n, slots, *refs):
    hbm = dict(zip(LOCAL, refs[: len(LOCAL)]))
    out_layer, out_state = refs[len(LOCAL) : len(LOCAL) + 2]
    refs = refs[len(LOCAL) + 2 :]
    ref = dict(zip(LOCAL, refs[: len(LOCAL)]))
    (
        q_all, sel_buf, msg, inbox, m_send, m_recv, a_send, a_recv, q_slot, o_slot, y_v,
        keys, values, scores_v, weights_v, stat_v,
        in_sem, send_sem, recv_sem, z_sem,
    ) = refs[len(LOCAL) :]
    me = lax.axis_index("req")
    tp = lax.axis_index("tp")

    copies = {}
    for k, name in enumerate(LOCAL):
        dst = ref[name].at[pl.ds(0, HEADS * HD)] if name == "wq" else ref[name]
        copies[name] = pltpu.make_async_copy(hbm[name], dst, in_sem.at[k])
        copies[name].start()

    z_n = depth_of(n)
    plane_n = n // z_n
    core = lax.rem(me, 2)
    z = lax.rem(me // 2, z_n)
    place = me // (2 * z_n) * 2 + core

    def at(place, z):
        return place // 2 * (2 * z_n) + z * 2 + lax.rem(place, 2)

    z_order = sorted(range(1, z_n), key=lambda i: (min(i, z_n - i), i))
    column = {i: at(place, lax.rem(z + i, z_n)) for i in z_order}
    plane = [at(lax.rem(place + j, plane_n), z) for j in range(1, plane_n)]

    barrier = pltpu.get_barrier_semaphore()
    for i in reversed(z_order):
        pl.semaphore_signal(barrier, inc=1, device_id={"req": column[i]})
    for d in plane:
        pl.semaphore_signal(barrier, inc=1, device_id={"req": d})
    for i in range(1, tp_n):
        pl.semaphore_signal(barrier, inc=1, device_id={"tp": lax.rem(tp + i, tp_n)})
    inbox[...] = jnp.zeros_like(inbox)
    o_slot[...] = jnp.zeros_like(o_slot)
    q_slot[...] = jnp.zeros_like(q_slot)
    block = ref["cache"].shape[1]
    quad_n = (slots + 3) // 4

    def tp_start(src, dst, k):
        for i in range(1, tp_n):
            p = lax.rem(tp + i, tp_n)
            pltpu.make_async_remote_copy(
                src_ref=src(p), dst_ref=dst.at[tp], send_sem=send_sem.at[k], recv_sem=recv_sem.at[k],
                device_id={"tp": p},
            ).start()

    def wait_all(buf, k, count, which):
        view = buf.at[pl.ds(0, count), pl.ds(0, 6)] if k == 3 else buf.at[pl.ds(0, count)]
        copy = pltpu.make_async_remote_copy(
            src_ref=view, dst_ref=view, send_sem=send_sem.at[k], recv_sem=recv_sem.at[k], device_id={"tp": tp}
        )
        if which == "send":
            copy.wait_send()
        else:
            copy.wait_recv()

    lane8 = iota((ROWS, LANES), 1)
    low8 = lane8 < HD

    ref["wq"][pl.ds(HEADS * HD, 64), :] = jnp.zeros((64, ref["wq"].shape[1]), BF16)
    copies["hidden"].wait()
    copies["gain"].wait()
    hidden = ref["hidden"][...].astype(F32)
    width = hidden.shape[1]
    mean = jnp.sum(hidden * hidden, axis=1, keepdims=True) * (1.0 / width)
    normed = (hidden * lax.rsqrt(mean + 1e-06) * ref["gain"][...].reshape(1, width)).astype(BF16)

    for name in ("len_s", "sr_s", "sb_s", "freq"):
        copies[name].wait()
    position = jnp.zeros((ROWS, LANES), F32)
    row8 = iota((ROWS, LANES), 0)
    for r in range(ROWS):
        position = jnp.where(row8 == r, ref["len_s"][me * ROWS + r].astype(F32), position)
    angles = position * ref["freq"][...]
    cosine = jnp.cos(angles)
    sine = jnp.sin(angles)
    front = (lane8 & (HD - 1)) < HD // 2

    def rot(v):
        other = jnp.where(front, -pltpu.roll(v, LANES - HD // 2, 1), pltpu.roll(v, HD // 2, 1))
        return v * cosine + other * sine

    copies["wq"].wait()
    q_raw = dot_nt(normed, ref["wq"][...])
    query = [rot(q_raw[:, c * LANES : (c + 1) * LANES]).astype(BF16) for c in range(3)]
    for c in range(3):
        q_all[me, :, c * LANES : (c + 1) * LANES] = query[c]

    pl.semaphore_wait(barrier, len(z_order) + len(plane) + tp_n - 1)

    def z_copy(i, source, target):
        return pltpu.make_async_remote_copy(
            src_ref=q_all.at[source], dst_ref=q_all.at[source], send_sem=send_sem.at[0], recv_sem=z_sem.at[i - 1],
            device_id={"req": target},
        )

    def pass_on(source):
        for d in plane:
            pltpu.make_async_remote_copy(
                src_ref=q_all.at[source], dst_ref=q_all.at[source], send_sem=send_sem.at[0], recv_sem=recv_sem.at[0],
                device_id={"req": d},
            ).start()

    def pass_on_from(distance):
        for i in z_order:
            if min(i, z_n - i) == distance:
                source = at(place, lax.rem(z + z_n - i, z_n))
                z_copy(i, source, source).wait_recv()
                pass_on(source)

    for i in reversed(z_order):
        z_copy(i, me, column[i]).start()
    pass_on(me)

    copies["mi"].wait()
    mamba_x = dot_nt(normed, ref["mi"][0]).astype(BF16)
    for name in ("cw", "cs", "sw"):
        copies[name].wait()
    taps = ref["cw"].shape[0]
    conv = ref["cw"][taps - 1 : taps, :] * mamba_x.astype(F32)
    for j in range(taps - 1):
        conv = conv + ref["cw"][j : j + 1, :] * ref["cs"][j].astype(F32)
    activated = silu(conv).astype(BF16)
    part = dot_nt(activated, ref["sw"][...])
    sel_buf[tp] = jnp.concatenate([part, jnp.zeros((ROWS, 2 * LANES - part.shape[1]), F32)], axis=1)
    tp_start(lambda p: sel_buf.at[tp], sel_buf, 1)

    def pack(quads):
        for g in quads:
            for c in range(2):
                s0 = 4 * g + 2 * c
                lanes = slice(c * LANES, (c + 1) * LANES)
                if s0 < slots:
                    one, two = ref["cache"][s0], ref["cache"][s0 + 1]
                    keys[g, :, lanes] = jnp.concatenate([one[:, 0:HD], two[:, 0:HD]], axis=1)
                    values[g, :, lanes] = jnp.concatenate([one[:, HD:], two[:, HD:]], axis=1)
                else:
                    keys[g, :, lanes] = jnp.zeros((block, LANES), BF16)
                    values[g, :, lanes] = jnp.zeros((block, LANES), BF16)

    pass_on_from(1)
    copies["cache"].wait()
    third = quad_n // 3
    pack(range(0, third))
    pass_on_from(2)
    pack(range(third, 2 * third))
    pass_on_from(3)
    pack(range(2 * third, quad_n))
    lane40 = lax.rem(lane8, SPAD)
    lane40 = jnp.where(lane8 < 3 * SPAD, lane40, -1)
    sr_row = jnp.full((ROWS, LANES), -1, jnp.int32)
    sub_col = iota((SPAD, LANES), 0)
    sr_col = jnp.full((SPAD, LANES), -1, jnp.int32)
    for s in range(slots):
        v = ref["sr_s"][s]
        sr_row = jnp.where(lane40 == s, v, sr_row)
        sr_col = jnp.where(sub_col == s, v, sr_col)
    dest_row = lax.shift_right_arithmetic(sr_row, 3)
    rank_row = jnp.zeros((ROWS, LANES), jnp.int32)
    for s in range(slots):
        d = lax.shift_right_arithmetic(ref["sr_s"][s], 3)
        rank_row = rank_row + jnp.where((dest_row == d) & (lane40 > s), 1, 0)
    m_rows = n * 8
    mr = iota((m_rows, LANES), 0)
    mj = lax.shift_right_arithmetic(mr & 7, 1)
    cj = jnp.where(lane8 < SPAD, 0, jnp.where(lane8 < 2 * SPAD, 1, jnp.where(lane8 < 3 * SPAD, 2, -1)))
    pick = (
        (lax.shift_right_arithmetic(mr, 3) == dest_row[0:1, :])
        & ((mr & 1) == rank_row[0:1, :])
        & (mj == cj[0:1, :])
    )
    pick = jnp.where(pick, 1.0, 0.0).astype(BF16)
    own_pick = jnp.concatenate([sr_col] * (n * 8 // LANES), axis=1) if n * 8 >= LANES else sr_col[:, 0 : n * 8]
    own_pick = jnp.where(own_pick == iota((SPAD, n * 8), 1), 1.0, 0.0).astype(BF16)

    for distance in range(4, z_n // 2 + 1):
        pass_on_from(distance)
    wait_all(q_all, 0, n - z_n, "recv")
    q_sel = dot(own_pick, q_all[...].reshape(n * 8, 3 * LANES))
    low40 = iota((SPAD, LANES), 1) < HD
    for h in range(HEADS):
        col = q_sel[:, (h // 2) * LANES : (h // 2 + 1) * LANES]
        turn = pltpu.roll(col, HD, 1)
        both = jnp.where(low40, col, turn) if h % 2 == 0 else jnp.where(low40, turn, col)
        q_slot[h * SPAD : (h + 1) * SPAD, :] = both * HD**-0.5
    time = iota((8, block), 1)

    def live(s):
        owner = ref["sr_s"][s]
        used = owner >= 0
        return jnp.where(used, ref["len_s"][jnp.where(used, owner, 0)] - ref["sb_s"][s] * block, 0)

    zero = jnp.zeros((8, LANES), F32)
    for g in range(quad_n):
        lhs = []
        for i in range(4):
            q = q_slot[pl.ds(4 * g + i, 8, stride=SPAD), :]
            q = jnp.where(low8, q, 0.0) if i % 2 == 0 else jnp.where(low8, 0.0, q)
            lhs.append(jnp.concatenate([q, zero] if i < 2 else [zero, q], axis=1))
        lhs = jnp.concatenate(lhs, axis=0).astype(BF16)
        scores_v[g] = dot_nt(lhs, keys[g])
    for g in range(quad_n):
        for i in range(4):
            s = 4 * g + i
            rows = slice(i * 8, i * 8 + 8)
            if s >= slots:
                weights_v[g, rows, :] = jnp.zeros((8, block), BF16)
                continue
            scores = jnp.where(time < live(s), scores_v[g, rows, :], NEG)
            top = jnp.max(scores, axis=1, keepdims=True)
            weights = jnp.exp(scores - top).astype(BF16)
            weights_v[g, rows, :] = weights
            total = jnp.sum(weights.astype(F32), axis=1, keepdims=True)
            stat_v[0, s] = jnp.broadcast_to(top + jnp.log(total), (8, LANES))
            stat_v[1, s] = jnp.broadcast_to(1.0 / total, (8, LANES))
    for g in range(quad_n):
        out = dot(weights_v[g], values[g])
        for i in range(4):
            s = 4 * g + i
            if s < slots:
                part = out[i * 8 : i * 8 + 8, (i // 2) * LANES : (i // 2 + 1) * LANES] * stat_v[1, s]
                lse = stat_v[0, s]
                part = jnp.where(low8, part, lse) if i % 2 == 0 else jnp.where(low8, lse, part)
                o_slot[pl.ds(s, 8, stride=SPAD), :] = part

    lane40v = iota((SPAD, LANES), 1)
    odd = (iota((SPAD, LANES), 0) & 1) == 1
    outs, turned = [], []
    for h in range(HEADS):
        one = o_slot[h * SPAD : (h + 1) * SPAD, :]
        two = pltpu.roll(one, HD, 1)
        outs.append(jnp.where(odd, one, two))
        turned.append(jnp.where(odd, two, one))
    tail = jnp.where(lane40v == 80, ((sr_col & 7) + 1).astype(F32), 0.0)
    for h in range(HEADS):
        rest = turned[h]
        for t in range(3):
            term = rest.astype(BF16).astype(F32)
            tail = jnp.where(lane40v == HD + 3 * h + t, term, tail)
            rest = rest - term
    table = jnp.concatenate(
        [
            jnp.where(low40, turned[0], outs[1]),
            jnp.where(low40, turned[2], outs[3]),
            jnp.where(low40, turned[4], tail),
            jnp.zeros((8, LANES), F32),
        ],
        axis=0,
    ).astype(BF16)
    msg[...] = dot(pick, table).reshape(n, 8, LANES).astype(BF16)
    inbox[me] = msg[me]

    for i in list(reversed(z_order)) + [0]:
        for j in reversed(range(plane_n)):
            if i or j:
                d = at(lax.rem(place + j, plane_n), lax.rem(z + i, z_n))
                pltpu.make_async_remote_copy(
                    src_ref=msg.at[d, pl.ds(0, 6)], dst_ref=inbox.at[me, pl.ds(0, 6)], send_sem=send_sem.at[3],
                    recv_sem=recv_sem.at[3], device_id={"req": d},
                ).start()

    gate = silu(dot_nt(normed, ref["mi"][1]))
    copies["wm"].wait()
    memory = dot(normed, ref["wm"][...])
    key_value = jnp.where(low8, rot(memory), memory).astype(BF16).astype(F32)
    swapped = pltpu.roll(key_value, HD, 1)
    key_both = jnp.where(low8, key_value, swapped)
    value_both = jnp.where(low8, swapped, key_value)

    own_score = []
    for h in range(HEADS):
        half = low8 if h % 2 == 0 else jnp.logical_not(low8)
        prod = jnp.where(half, query[h // 2].astype(F32) * key_both, 0.0)
        own_score.append(jnp.sum(prod, axis=1, keepdims=True) * HD**-0.5)

    wait_all(sel_buf, 1, tp_n - 1, "recv")
    selection = sel_buf[0]
    for p in range(1, tp_n):
        selection = selection + sel_buf[p]
    dtr = ref["st"].shape[1]
    ns = ref["dl"].shape[0]
    for name in ("st", "sb", "dl", "sg", "ss", "mg", "mo"):
        copies[name].wait()
    step = softplus(dot_nt(selection[:, 0:dtr].astype(BF16), ref["st"][...]) + ref["sb"][...])
    maps = pltpu.roll(selection, selection.shape[1] - dtr, 1)[:, 0:LANES]
    maps = jnp.transpose(maps)
    active = activated.astype(F32)
    decay = jnp.exp(ref["dl"][...])
    drive = step * active
    for r in range(ROWS):
        new = (
            jnp.exp(-step[r : r + 1, :] * decay) * ref["ss"][r]
            + drive[r : r + 1, :] * maps[0:ns, r : r + 1]
        )
        out_state[r] = new
        y_v[r : r + 1, :] = jnp.sum(maps[ns : 2 * ns, r : r + 1] * new, axis=0, keepdims=True)
    mamba_y = (y_v[...] + ref["sg"][...] * active) * gate

    def share(used, weight, square, send, recv, k):
        proj = dot(used, weight)
        extra = jnp.zeros((ROWS, 13 * LANES - proj.shape[1]), F32)
        proj = jnp.concatenate([proj, extra], axis=1)
        tail = iota((ROWS, TP_PAD), 1) >= TP_COLS
        for p in range(tp_n):
            moved = proj if p == 0 else pltpu.roll(proj, proj.shape[1] - p * TP_COLS, 1)
            send[p] = jnp.where(tail, square, moved[:, 0:TP_PAD])
        recv[tp] = send[tp]
        tp_start(lambda p: send.at[p], recv, k)

    def gathered(recv, k):
        wait_all(recv, k, tp_n - 1, "recv")
        total = recv[0]
        for p in range(1, tp_n):
            total = total + recv[p]
        return total

    mamba_square = jnp.sum(mamba_y * mamba_y, axis=1, keepdims=True)
    share((mamba_y * ref["mg"][...]).astype(BF16), ref["mo"][...], mamba_square, m_send, m_recv, 2)

    wide = jnp.concatenate([hidden, jnp.zeros((ROWS, 13 * LANES - width), F32)], axis=1)
    residual = wide[:, 0:TP_PAD]
    for p in range(1, tp_n):
        residual = jnp.where(tp == p, pltpu.roll(wide, wide.shape[1] - p * TP_COLS, 1)[:, 0:TP_PAD], residual)
    e_row = iota((16, LANES), 0)
    e_lane = iota((16, LANES), 1)
    e_start = HD + 3 * e_row
    spread_rows = ((e_row < HEADS) & (e_lane >= e_start) & (e_lane < e_start + 3)) | ((e_row == HEADS) & (e_lane == 80))
    spread_rows = jnp.where(spread_rows, 1.0, 0.0).astype(BF16)
    copies["ag"].wait()
    copies["wo"].wait()

    wait_all(inbox, 3, n - 1, "recv")
    box = inbox[...].reshape(n * 8, LANES)
    heads_row = dot_nt(spread_rows, box)
    col_j = lax.shift_right_arithmetic(iota((ROWS, n * 8), 1) & 7, 1)
    r_id = (iota((ROWS, n * 8), 0) + 1).astype(F32)
    shifted = [pltpu.roll(heads_row, n * 8 - (4 - 2 * j), 1) if j < 2 else heads_row for j in range(3)]
    high, low, den, own_w = [], [], [], []
    for h in range(HEADS):
        j = h // 2
        lse = jnp.broadcast_to(shifted[j][h : h + 1, :], (ROWS, n * 8))
        rid = jnp.broadcast_to(shifted[j][HEADS : HEADS + 1, :], (ROWS, n * 8))
        mine = (rid == r_id) & (col_j == j)
        top = jnp.maximum(jnp.max(jnp.where(mine, lse, NEG), axis=1, keepdims=True), own_score[h])
        w = jnp.where(mine, jnp.exp(lse - top), 0.0)
        own = jnp.exp(own_score[h] - top)
        den.append(jnp.sum(w, axis=1, keepdims=True) + own)
        own_w.append(own)
        w_high = w.astype(BF16).astype(F32)
        high.append(w_high)
        low.append(w - w_high)
    merged = dot(jnp.concatenate(high + low, axis=0).astype(BF16), box)
    numer = [
        merged[h * 8 : h * 8 + 8] + merged[(HEADS + h) * 8 : (HEADS + h) * 8 + 8] + own_w[h] * value_both
        for h in range(HEADS)
    ]
    normal = [numer[h] / den[h] for h in range(HEADS)]
    attention = jnp.concatenate(
        [
            jnp.where(low8, normal[0], normal[1]),
            jnp.where(low8, normal[2], normal[3]),
            jnp.where(low8, normal[4], 0.0),
        ],
        axis=1,
    )[:, 0 : HEADS * HD]
    attn_square = jnp.sum(attention * attention, axis=1, keepdims=True)
    share((attention * ref["ag"][...].reshape(1, HEADS * HD)).astype(BF16), ref["wo"][...], attn_square, a_send, a_recv, 4)
    mamba = gathered(m_recv, 2)
    mamba_scale = jnp.sqrt(mamba[:, TP_COLS : TP_COLS + 1] * (1.0 / (TP_COLS * tp_n)) + 1e-06)
    base = residual + 0.5 * (mamba / mamba_scale)
    attn = gathered(a_recv, 4)
    attn_scale = jnp.sqrt(attn[:, TP_COLS : TP_COLS + 1] * (1.0 / (HEADS * HD * tp_n)) + 1e-06)
    final = base + 0.5 * (attn / attn_scale)
    out_layer[...] = final[:, 0:TP_COLS].astype(BF16)
    wait_all(q_all, 0, n - 1, "send")
    wait_all(sel_buf, 1, tp_n - 1, "send")
    wait_all(m_send, 2, tp_n - 1, "send")
    wait_all(msg, 3, n - 1, "send")
    wait_all(a_send, 4, tp_n - 1, "send")


def write_out(layer, state, layer_out, state_out, sem):
    first = pltpu.make_async_copy(state, state_out, sem.at[0])
    second = pltpu.make_async_copy(layer, layer_out, sem.at[1])
    first.start()
    second.start()
    first.wait()
    second.wait()


def body(
    hidden_in, norm_gain, query_weight, memory_weight, attention_out, attention_gain, mamba_input, conv_weight,
    conv_state, select_weight, step_weight, step_bias, decay_log, skip_gain, scan_state, mamba_gain, mamba_out,
    cache_blocks, lengths, slot_request, slot_block,
):
    n = lax.axis_size("req")
    tp_n = lax.axis_size("tp")
    slots, _, block, kv = cache_blocks.shape
    quad_n = (slots + 3) // 4
    rate = 10000.0 ** (-(np.arange(LANES) % (HD // 2)) * (2.0 / HD))
    freq = jnp.asarray(np.broadcast_to(rate[None, :], (ROWS, LANES)), F32)
    row = lambda v: v.reshape(1, -1)
    operand = {
        "len_s": lengths,
        "sr_s": slot_request,
        "sb_s": slot_block,
        "hidden": hidden_in,
        "gain": norm_gain,
        "freq": freq,
        "wq": query_weight.T,
        "wm": memory_weight,
        "mi": jnp.transpose(mamba_input, (0, 2, 1)),
        "cw": conv_weight,
        "cs": jnp.transpose(conv_state, (1, 0, 2)),
        "sw": select_weight.T,
        "st": step_weight.T,
        "sb": row(step_bias),
        "dl": decay_log,
        "sg": row(skip_gain),
        "ss": scan_state,
        "mg": row(mamba_gain),
        "mo": mamba_out,
        "cache": cache_blocks.reshape(slots, block, kv),
        "ag": attention_gain,
        "wo": attention_out,
    }
    operand = [pltpu.with_memory_space_constraint(operand[name], pltpu.HBM) for name in LOCAL]
    scratch = []
    for name, v in zip(LOCAL, operand):
        space = pltpu.SMEM if name in ("len_s", "sr_s", "sb_s") else pltpu.VMEM
        shape = (v.shape[0] + 64, v.shape[1]) if name == "wq" else v.shape
        scratch.append(space(shape, v.dtype))
    scratch += [
        pltpu.VMEM((n, ROWS, 3 * LANES), BF16),
        pltpu.VMEM((tp_n, ROWS, 2 * LANES), F32),
        pltpu.VMEM((n, 8, LANES), BF16),
        pltpu.VMEM((n, 8, LANES), BF16),
        pltpu.VMEM((tp_n, ROWS, TP_PAD), F32),
        pltpu.VMEM((tp_n, ROWS, TP_PAD), F32),
        pltpu.VMEM((tp_n, ROWS, TP_PAD), F32),
        pltpu.VMEM((tp_n, ROWS, TP_PAD), F32),
        pltpu.VMEM((8 * SPAD, LANES), F32),
        pltpu.VMEM((8 * SPAD, LANES), F32),
        pltpu.VMEM((ROWS, TP_COLS), F32),
        pltpu.VMEM((quad_n, block, 2 * LANES), BF16),
        pltpu.VMEM((quad_n, block, 2 * LANES), BF16),
        pltpu.VMEM((quad_n, 32, block), F32),
        pltpu.VMEM((quad_n, 32, block), BF16),
        pltpu.VMEM((2, slots, 8, LANES), F32),
        pltpu.SemaphoreType.DMA((len(LOCAL),)),
        pltpu.SemaphoreType.DMA((5,)),
        pltpu.SemaphoreType.DMA((5,)),
        pltpu.SemaphoreType.DMA((max(1, depth_of(n) - 1),)),
    ]

    def step(*refs):
        kernel(n, tp_n, slots, *refs)

    layer, state = pl.pallas_call(
        step,
        out_shape=(
            jax.ShapeDtypeStruct((ROWS, TP_COLS), BF16),
            jax.ShapeDtypeStruct(scan_state.shape, F32),
        ),
        in_specs=[pl.BlockSpec(memory_space=pltpu.HBM)] * len(operand),
        out_specs=(pl.BlockSpec(memory_space=pltpu.VMEM),) * 2,
        scratch_shapes=scratch,
        compiler_params=pltpu.CompilerParams(collective_id=0, has_side_effects=True, vmem_limit_bytes=24 << 20),
        name="decode_layer",
    )(*operand)
    results = (jax.ShapeDtypeStruct(layer.shape, BF16), jax.ShapeDtypeStruct(state.shape, F32))
    return pl.pallas_call(
        write_out,
        out_shape=results,
        in_specs=[pl.BlockSpec(memory_space=pltpu.VMEM)] * 2,
        out_specs=(pl.BlockSpec(memory_space=pl.ANY),) * 2,
        scratch_shapes=[pltpu.SemaphoreType.DMA((2,))],
        compiler_params=pltpu.CompilerParams(vmem_limit_bytes=1 << 20),
        name="write_out",
    )(layer, state)


def solution(mesh):
    return jax.shard_map(
        body,
        mesh=mesh,
        in_specs=(
            P("req", None),
            P(),
            P(None, "tp"),
            P(None, "tp"),
            P("tp", None),
            P("tp"),
            P(None, None, "tp"),
            P(None, "tp"),
            P("req", None, "tp"),
            P("tp", None),
            P(None, "tp"),
            P("tp"),
            P(None, "tp"),
            P("tp"),
            P("req", None, "tp"),
            P("tp"),
            P("tp", None),
            P("req", "tp", None, None),
            P(),
            P("req"),
            P("req"),
        ),
        out_specs=(P("req", "tp"), P("req", None, "tp")),
        check_vma=False,
    )
```

```python
import math

import jax
import jax.numpy as jnp
import numpy as np
from jax import lax
from jax.experimental import pallas as pl
from jax.experimental.pallas import tpu as pltpu
from jax.sharding import PartitionSpec as P

F32 = jnp.float32
BF16 = jnp.bfloat16
NEG = -1e30
ROWS = 8
HEADS = 5
HD = 64
LANES = 128
SPAD = 40
TP_COLS = 400
TP_PAD = 512
NT = (((1,), (1,)), ((), ()))


def depth_of(n):
    return 8 if n >= 32 else n // 4


def iota(shape, axis):
    return lax.broadcasted_iota(jnp.int32, shape, axis)


def dot(a, b):
    return jnp.dot(a, b, preferred_element_type=F32)


def dot_nt(a, b):
    return lax.dot_general(a, b, NT, preferred_element_type=F32)


def silu(v):
    return v * (1.0 / (1.0 + jnp.exp(-v)))


def softplus(v):
    return jnp.maximum(v, 0.0) + jnp.log1p(jnp.exp(-jnp.abs(v)))


LOCAL = (
    "len_s", "sr_s", "sb_s", "hidden", "gain", "freq", "wq", "wm", "mi", "cw", "cs", "sw", "st", "sb", "dl", "sg",
    "ss", "mg", "mo", "cache", "ag", "wo",
)


def kernel(n, tp_n, slots, *refs):
    hbm = dict(zip(LOCAL, refs[: len(LOCAL)]))
    out_layer, out_state = refs[len(LOCAL) : len(LOCAL) + 2]
    refs = refs[len(LOCAL) + 2 :]
    ref = dict(zip(LOCAL, refs[: len(LOCAL)]))
    (
        q_all, sel_buf, msg, inbox, m_send, m_recv, a_send, a_recv, q_slot, o_slot, y_v,
        keys, values, scores_v, weights_v, stat_v, pick,
        in_sem, send_sem, recv_sem, z_sem,
    ) = refs[len(LOCAL) :]
    me = lax.axis_index("req")
    tp = lax.axis_index("tp")

    z_n = depth_of(n)
    plane_n = n // z_n
    x_n = plane_n // 2
    core = lax.rem(me, 2)
    z = lax.rem(lax.div(me, 2), z_n)
    x = lax.div(me, 2 * z_n)

    def ahead(at, by, count, stride):
        return jnp.where(at >= count - by, (by - count) * stride, by * stride) if by else 0

    z_order = sorted(range(1, z_n), key=lambda i: (min(i, z_n - i), i))
    z_step = {i: ahead(z, i, z_n, 2) for i in range(z_n)}
    column = {i: me + z_step[i] for i in z_order}
    x_step = {i: ahead(x, i, x_n, 2 * z_n) for i in range(x_n)}
    core_step = {0: 0, 1: 1 - 2 * core}
    plane_order = sorted(range(1, plane_n), key=lambda j: -min(j // 2, x_n - j // 2))
    plane_step = [x_step[j // 2] + core_step[j % 2] for j in plane_order]
    plane = [me + step for step in plane_step]
    tp_peer = [tp + ahead(tp, i, tp_n, 1) for i in sorted(range(1, tp_n), key=lambda i: -min(i, tp_n - i))]

    barrier = pltpu.get_barrier_semaphore()
    for i in reversed(z_order):
        pl.semaphore_signal(barrier, inc=1, device_id={"req": column[i]})
    for d in plane:
        pl.semaphore_signal(barrier, inc=1, device_id={"req": d})
    for p in tp_peer:
        pl.semaphore_signal(barrier, inc=1, device_id={"tp": p})
    copies = {}
    for k, name in enumerate(LOCAL):
        dst = ref[name].at[pl.ds(0, HEADS * HD)] if name == "wq" else ref[name]
        copies[name] = pltpu.make_async_copy(hbm[name], dst, in_sem.at[k])
        copies[name].start()

    inbox[...] = jnp.zeros_like(inbox)
    o_slot[...] = jnp.zeros_like(o_slot)
    q_slot[...] = jnp.zeros_like(q_slot)
    block = ref["cache"].shape[1]
    quad_n = (slots + 3) // 4

    def tp_start(src, dst, k):
        for p in tp_peer:
            pltpu.make_async_remote_copy(
                src_ref=src(p), dst_ref=dst.at[tp], send_sem=send_sem.at[k], recv_sem=recv_sem.at[k],
                device_id={"tp": p},
            ).start()

    def wait_all(buf, k, count, which):
        view = buf.at[pl.ds(0, count), pl.ds(0, 6)] if k == 3 else buf.at[pl.ds(0, count)]
        copy = pltpu.make_async_remote_copy(
            src_ref=view, dst_ref=view, send_sem=send_sem.at[k], recv_sem=recv_sem.at[k], device_id={"tp": tp}
        )
        if which == "send":
            copy.wait_send()
        else:
            copy.wait_recv()

    lane8 = iota((ROWS, LANES), 1)
    low8 = lane8 < HD

    ref["wq"][pl.ds(HEADS * HD, 64), :] = jnp.zeros((64, ref["wq"].shape[1]), BF16)
    copies["hidden"].wait()
    copies["gain"].wait()
    hidden = ref["hidden"][...].astype(F32)
    width = hidden.shape[1]
    mean = jnp.sum(hidden * hidden, axis=1, keepdims=True) * (1.0 / width)
    normed = (hidden * lax.rsqrt(mean + 1e-06) * ref["gain"][...].reshape(1, width)).astype(BF16)

    for name in ("len_s", "sr_s", "sb_s", "freq"):
        copies[name].wait()
    position = jnp.zeros((ROWS, LANES), F32)
    row8 = iota((ROWS, LANES), 0)
    for r in range(ROWS):
        position = jnp.where(row8 == r, ref["len_s"][me * ROWS + r].astype(F32), position)
    angles = position * ref["freq"][...]
    cosine = jnp.cos(angles)
    sine = jnp.sin(angles)
    front = (lane8 & (HD - 1)) < HD // 2

    def rot(v):
        other = jnp.where(front, -pltpu.roll(v, LANES - HD // 2, 1), pltpu.roll(v, HD // 2, 1))
        return v * cosine + other * sine

    copies["wq"].wait()
    q_raw = dot_nt(normed, ref["wq"][...])
    query = [rot(q_raw[:, c * LANES : (c + 1) * LANES]).astype(BF16) for c in range(3)]
    for c in range(3):
        q_all[me, :, c * LANES : (c + 1) * LANES] = query[c]

    pl.semaphore_wait(barrier, len(z_order) + len(plane) + tp_n - 1)

    def z_copy(i, source, target):
        return pltpu.make_async_remote_copy(
            src_ref=q_all.at[source], dst_ref=q_all.at[source], send_sem=send_sem.at[0], recv_sem=z_sem.at[i - 1],
            device_id={"req": target},
        )

    def pass_on(source):
        for d in plane:
            pltpu.make_async_remote_copy(
                src_ref=q_all.at[source], dst_ref=q_all.at[source], send_sem=send_sem.at[0], recv_sem=recv_sem.at[0],
                device_id={"req": d},
            ).start()

    def pass_on_from(distance):
        for i in z_order:
            if min(i, z_n - i) == distance:
                source = column[z_n - i]
                z_copy(i, source, source).wait_recv()
                pass_on(source)

    for i in reversed(z_order):
        z_copy(i, me, column[i]).start()
    pass_on(me)

    copies["mi"].wait()
    mamba_x = dot_nt(normed, ref["mi"][0]).astype(BF16)
    for name in ("cw", "cs", "sw"):
        copies[name].wait()
    taps = ref["cw"].shape[0]
    conv = ref["cw"][taps - 1 : taps, :] * mamba_x.astype(F32)
    for j in range(taps - 1):
        conv = conv + ref["cw"][j : j + 1, :] * ref["cs"][j].astype(F32)
    activated = silu(conv).astype(BF16)
    part = dot_nt(activated, ref["sw"][...])
    sel_buf[tp] = jnp.concatenate([part, jnp.zeros((ROWS, 2 * LANES - part.shape[1]), F32)], axis=1)
    tp_start(lambda p: sel_buf.at[tp], sel_buf, 1)

    def pack(quads):
        for g in quads:
            for c in range(2):
                s0 = 4 * g + 2 * c
                lanes = slice(c * LANES, (c + 1) * LANES)
                if s0 < slots:
                    one, two = ref["cache"][s0], ref["cache"][s0 + 1]
                    keys[g, :, lanes] = jnp.concatenate([one[:, 0:HD], two[:, 0:HD]], axis=1)
                    values[g, :, lanes] = jnp.concatenate([one[:, HD:], two[:, HD:]], axis=1)
                else:
                    keys[g, :, lanes] = jnp.zeros((block, LANES), BF16)
                    values[g, :, lanes] = jnp.zeros((block, LANES), BF16)

    pass_on_from(1)
    copies["cache"].wait()
    third = quad_n // 3
    pack(range(0, third))
    for distance in range(2, z_n // 2 + 1):
        pass_on_from(distance)
    pack(range(third, quad_n))
    lane40 = lax.rem(lane8, SPAD)
    lane40 = jnp.where(lane8 < 3 * SPAD, lane40, -1)
    sr_row = jnp.full((ROWS, LANES), -1, jnp.int32)
    sub_col = iota((SPAD, LANES), 0)
    sr_col = jnp.full((SPAD, LANES), -1, jnp.int32)
    for s in range(slots):
        v = ref["sr_s"][s]
        sr_row = jnp.where(lane40 == s, v, sr_row)
        sr_col = jnp.where(sub_col == s, v, sr_col)
    dest_row = lax.shift_right_arithmetic(sr_row, 3)
    rank_row = jnp.zeros((ROWS, LANES), jnp.int32)
    for s in range(slots):
        d = lax.shift_right_arithmetic(ref["sr_s"][s], 3)
        rank_row = rank_row + jnp.where((dest_row == d) & (lane40 > s), 1, 0)
    mr = iota((8, LANES), 0)
    cj = jnp.where(lane8 < SPAD, 0, jnp.where(lane8 < 2 * SPAD, 1, jnp.where(lane8 < 3 * SPAD, 2, -1)))
    fits = ((mr & 1) == rank_row) & (lax.shift_right_arithmetic(mr, 1) == cj)
    dests = [me + (z_step[i] + step) for i in list(reversed(z_order)) + [0] for step in plane_step + [0]]
    for k, d in enumerate(dests):
        pick[k * 8 : (k + 1) * 8, :] = jnp.where(fits & (dest_row == d), 1.0, 0.0)
    own_pick = jnp.concatenate([sr_col] * (n * 8 // LANES), axis=1) if n * 8 >= LANES else sr_col[:, 0 : n * 8]
    own_pick = jnp.where(own_pick == iota((SPAD, n * 8), 1), 1.0, 0.0).astype(BF16)

    wait_all(q_all, 0, n - z_n, "recv")
    q_sel = dot(own_pick, q_all[...].reshape(n * 8, 3 * LANES))
    low40 = iota((SPAD, LANES), 1) < HD
    for h in range(HEADS):
        col = q_sel[:, (h // 2) * LANES : (h // 2 + 1) * LANES]
        turn = pltpu.roll(col, HD, 1)
        both = jnp.where(low40, col, turn) if h % 2 == 0 else jnp.where(low40, turn, col)
        q_slot[h * SPAD : (h + 1) * SPAD, :] = both * HD**-0.5
    time = iota((8, block), 1)

    def live(s):
        owner = ref["sr_s"][s]
        used = owner >= 0
        return jnp.where(used, ref["len_s"][jnp.where(used, owner, 0)] - ref["sb_s"][s] * block, 0)

    zero = jnp.zeros((8, LANES), F32)
    for g in range(quad_n):
        lhs = []
        for i in range(4):
            q = q_slot[pl.ds(4 * g + i, 8, stride=SPAD), :]
            q = jnp.where(low8, q, 0.0) if i % 2 == 0 else jnp.where(low8, 0.0, q)
            lhs.append(jnp.concatenate([q, zero] if i < 2 else [zero, q], axis=1))
        lhs = jnp.concatenate(lhs, axis=0).astype(BF16)
        scores_v[g] = dot_nt(lhs, keys[g])
    for g in range(quad_n):
        for i in range(4):
            s = 4 * g + i
            rows = slice(i * 8, i * 8 + 8)
            if s >= slots:
                weights_v[g, rows, :] = jnp.zeros((8, block), BF16)
                continue
            scores = jnp.where(time < live(s), scores_v[g, rows, :], NEG)
            top = jnp.max(scores, axis=1, keepdims=True)
            weights = jnp.exp(scores - top).astype(BF16)
            weights_v[g, rows, :] = weights
            total = jnp.sum(weights.astype(F32), axis=1, keepdims=True)
            stat_v[0, s] = jnp.broadcast_to(top + jnp.log(total), (8, LANES))
            stat_v[1, s] = jnp.broadcast_to(1.0 / total, (8, LANES))
    for g in range(quad_n):
        out = dot(weights_v[g], values[g])
        for i in range(4):
            s = 4 * g + i
            if s < slots:
                part = out[i * 8 : i * 8 + 8, (i // 2) * LANES : (i // 2 + 1) * LANES] * stat_v[1, s]
                lse = stat_v[0, s]
                part = jnp.where(low8, part, lse) if i % 2 == 0 else jnp.where(low8, lse, part)
                o_slot[pl.ds(s, 8, stride=SPAD), :] = part

    lane40v = iota((SPAD, LANES), 1)
    odd = (iota((SPAD, LANES), 0) & 1) == 1
    outs, turned = [], []
    for h in range(HEADS):
        one = o_slot[h * SPAD : (h + 1) * SPAD, :]
        two = pltpu.roll(one, HD, 1)
        outs.append(jnp.where(odd, one, two))
        turned.append(jnp.where(odd, two, one))
    tail = jnp.where(lane40v == 80, ((sr_col & 7) + 1).astype(F32), 0.0)
    for h in range(HEADS):
        rest = turned[h]
        for t in range(3):
            term = rest.astype(BF16).astype(F32)
            tail = jnp.where(lane40v == HD + 3 * h + t, term, tail)
            rest = rest - term
    table = jnp.concatenate(
        [
            jnp.where(low40, turned[0], outs[1]),
            jnp.where(low40, turned[2], outs[3]),
            jnp.where(low40, turned[4], tail),
            jnp.zeros((8, LANES), F32),
        ],
        axis=0,
    ).astype(BF16)
    part_n = n // 4
    for c in range(4):
        rows = pick[c * part_n * 8 : (c + 1) * part_n * 8, :].astype(BF16)
        msg[c * part_n : (c + 1) * part_n] = dot(rows, table).reshape(part_n, 8, LANES).astype(BF16)
        for k in range(c * part_n, min((c + 1) * part_n, n - 1)):
            pltpu.make_async_remote_copy(
                src_ref=msg.at[k, pl.ds(0, 6)], dst_ref=inbox.at[me, pl.ds(0, 6)], send_sem=send_sem.at[3],
                recv_sem=recv_sem.at[3], device_id={"req": dests[k]},
            ).start()
    inbox[me] = msg[n - 1]

    gate = silu(dot_nt(normed, ref["mi"][1]))
    copies["wm"].wait()
    memory = dot(normed, ref["wm"][...])
    key_value = jnp.where(low8, rot(memory), memory).astype(BF16).astype(F32)
    swapped = pltpu.roll(key_value, HD, 1)
    key_both = jnp.where(low8, key_value, swapped)
    value_both = jnp.where(low8, swapped, key_value)

    own_score = []
    for h in range(HEADS):
        half = low8 if h % 2 == 0 else jnp.logical_not(low8)
        prod = jnp.where(half, query[h // 2].astype(F32) * key_both, 0.0)
        own_score.append(jnp.sum(prod, axis=1, keepdims=True) * HD**-0.5)

    wait_all(sel_buf, 1, tp_n - 1, "recv")
    selection = sel_buf[0]
    for p in range(1, tp_n):
        selection = selection + sel_buf[p]
    dtr = ref["st"].shape[1]
    ns = ref["dl"].shape[0]
    for name in ("st", "sb", "dl", "sg", "ss", "mg", "mo"):
        copies[name].wait()
    step = softplus(dot_nt(selection[:, 0:dtr].astype(BF16), ref["st"][...]) + ref["sb"][...])
    maps = pltpu.roll(selection, selection.shape[1] - dtr, 1)[:, 0:LANES]
    maps = jnp.transpose(maps)
    active = activated.astype(F32)
    decay = jnp.exp(ref["dl"][...])
    drive = step * active
    for r in range(ROWS):
        new = (
            jnp.exp(-step[r : r + 1, :] * decay) * ref["ss"][r]
            + drive[r : r + 1, :] * maps[0:ns, r : r + 1]
        )
        out_state[r] = new
        y_v[r : r + 1, :] = jnp.sum(maps[ns : 2 * ns, r : r + 1] * new, axis=0, keepdims=True)
    mamba_y = (y_v[...] + ref["sg"][...] * active) * gate

    def share(used, weight, square, send, recv, k):
        proj = dot(used, weight)
        extra = jnp.zeros((ROWS, 13 * LANES - proj.shape[1]), F32)
        proj = jnp.concatenate([proj, extra], axis=1)
        lane = iota((ROWS, TP_PAD), 1)
        terms, remain = jnp.zeros((ROWS, TP_PAD), F32), square
        for k_term in range(3):
            term = remain.astype(BF16).astype(F32)
            terms = jnp.where(lane == TP_COLS + k_term, term, terms)
            remain = remain - term
        for p in range(tp_n):
            moved = proj if p == 0 else pltpu.roll(proj, proj.shape[1] - p * TP_COLS, 1)
            send[p] = jnp.where(lane >= TP_COLS, terms, moved[:, 0:TP_PAD]).astype(send.dtype)
        recv[tp] = send[tp]
        tp_start(lambda p: send.at[p], recv, k)

    def gathered(recv, k):
        wait_all(recv, k, tp_n - 1, "recv")
        total = recv[0].astype(F32)
        for p in range(1, tp_n):
            total = total + recv[p].astype(F32)
        square = total[:, TP_COLS : TP_COLS + 1]
        for k_term in range(1, 3):
            square = square + total[:, TP_COLS + k_term : TP_COLS + k_term + 1]
        return total, square

    mamba_square = jnp.sum(mamba_y * mamba_y, axis=1, keepdims=True)
    share((mamba_y * ref["mg"][...]).astype(BF16), ref["mo"][...], mamba_square, m_send, m_recv, 2)

    wide = jnp.concatenate([hidden, jnp.zeros((ROWS, 13 * LANES - width), F32)], axis=1)
    residual = wide[:, 0:TP_PAD]
    for p in range(1, tp_n):
        residual = jnp.where(tp == p, pltpu.roll(wide, wide.shape[1] - p * TP_COLS, 1)[:, 0:TP_PAD], residual)
    e_row = iota((16, LANES), 0)
    e_lane = iota((16, LANES), 1)
    e_start = HD + 3 * e_row
    spread_rows = ((e_row < HEADS) & (e_lane >= e_start) & (e_lane < e_start + 3)) | ((e_row == HEADS) & (e_lane == 80))
    spread_rows = jnp.where(spread_rows, 1.0, 0.0).astype(BF16)
    copies["ag"].wait()
    copies["wo"].wait()

    wait_all(inbox, 3, n - 1, "recv")
    box = inbox[...].reshape(n * 8, LANES)
    heads_row = dot_nt(spread_rows, box)
    col_j = lax.shift_right_arithmetic(iota((ROWS, n * 8), 1) & 7, 1)
    r_id = (iota((ROWS, n * 8), 0) + 1).astype(F32)
    shifted = [pltpu.roll(heads_row, n * 8 - (4 - 2 * j), 1) if j < 2 else heads_row for j in range(3)]
    high, low, den, own_w = [], [], [], []
    for h in range(HEADS):
        j = h // 2
        lse = jnp.broadcast_to(shifted[j][h : h + 1, :], (ROWS, n * 8))
        rid = jnp.broadcast_to(shifted[j][HEADS : HEADS + 1, :], (ROWS, n * 8))
        mine = (rid == r_id) & (col_j == j)
        top = jnp.maximum(jnp.max(jnp.where(mine, lse, NEG), axis=1, keepdims=True), own_score[h])
        w = jnp.where(mine, jnp.exp(lse - top), 0.0)
        own = jnp.exp(own_score[h] - top)
        den.append(jnp.sum(w, axis=1, keepdims=True) + own)
        own_w.append(own)
        w_high = w.astype(BF16).astype(F32)
        high.append(w_high)
        low.append(w - w_high)
    merged = dot(jnp.concatenate(high + low, axis=0).astype(BF16), box)
    numer = [
        merged[h * 8 : h * 8 + 8] + merged[(HEADS + h) * 8 : (HEADS + h) * 8 + 8] + own_w[h] * value_both
        for h in range(HEADS)
    ]
    normal = [numer[h] / den[h] for h in range(HEADS)]
    attention = jnp.concatenate(
        [
            jnp.where(low8, normal[0], normal[1]),
            jnp.where(low8, normal[2], normal[3]),
            jnp.where(low8, normal[4], 0.0),
        ],
        axis=1,
    )[:, 0 : HEADS * HD]
    attn_square = jnp.sum(attention * attention, axis=1, keepdims=True)
    share((attention * ref["ag"][...].reshape(1, HEADS * HD)).astype(BF16), ref["wo"][...], attn_square, a_send, a_recv, 4)
    mamba, square = gathered(m_recv, 2)
    mamba_scale = jnp.sqrt(square * (1.0 / (TP_COLS * tp_n)) + 1e-06)
    base = residual + 0.5 * (mamba / mamba_scale)
    attn, square = gathered(a_recv, 4)
    attn_scale = jnp.sqrt(square * (1.0 / (HEADS * HD * tp_n)) + 1e-06)
    final = base + 0.5 * (attn / attn_scale)
    out_layer[...] = final[:, 0:TP_COLS].astype(BF16)
    wait_all(q_all, 0, n - 1, "send")
    wait_all(sel_buf, 1, tp_n - 1, "send")
    wait_all(m_send, 2, tp_n - 1, "send")
    wait_all(msg, 3, n - 1, "send")
    wait_all(a_send, 4, tp_n - 1, "send")


def write_out(layer, state, layer_out, state_out, sem):
    first = pltpu.make_async_copy(state, state_out, sem.at[0])
    second = pltpu.make_async_copy(layer, layer_out, sem.at[1])
    first.start()
    second.start()
    first.wait()
    second.wait()


def body(
    hidden_in, norm_gain, query_weight, memory_weight, attention_out, attention_gain, mamba_input, conv_weight,
    conv_state, select_weight, step_weight, step_bias, decay_log, skip_gain, scan_state, mamba_gain, mamba_out,
    cache_blocks, lengths, slot_request, slot_block,
):
    n = lax.axis_size("req")
    tp_n = lax.axis_size("tp")
    slots, _, block, kv = cache_blocks.shape
    quad_n = (slots + 3) // 4
    rate = 10000.0 ** (-(np.arange(LANES) % (HD // 2)) * (2.0 / HD))
    freq = jnp.asarray(np.broadcast_to(rate[None, :], (ROWS, LANES)), F32)
    row = lambda v: v.reshape(1, -1)
    operand = {
        "len_s": lengths,
        "sr_s": slot_request,
        "sb_s": slot_block,
        "hidden": hidden_in,
        "gain": norm_gain,
        "freq": freq,
        "wq": query_weight.T,
        "wm": memory_weight,
        "mi": jnp.transpose(mamba_input, (0, 2, 1)),
        "cw": conv_weight,
        "cs": jnp.transpose(conv_state, (1, 0, 2)),
        "sw": select_weight.T,
        "st": step_weight.T,
        "sb": row(step_bias),
        "dl": decay_log,
        "sg": row(skip_gain),
        "ss": scan_state,
        "mg": row(mamba_gain),
        "mo": mamba_out,
        "cache": cache_blocks.reshape(slots, block, kv),
        "ag": attention_gain,
        "wo": attention_out,
    }
    operand = [pltpu.with_memory_space_constraint(operand[name], pltpu.HBM) for name in LOCAL]
    scratch = []
    for name, v in zip(LOCAL, operand):
        space = pltpu.SMEM if name in ("len_s", "sr_s", "sb_s") else pltpu.VMEM
        shape = (v.shape[0] + 64, v.shape[1]) if name == "wq" else v.shape
        scratch.append(space(shape, v.dtype))
    scratch += [
        pltpu.VMEM((n, ROWS, 3 * LANES), BF16),
        pltpu.VMEM((tp_n, ROWS, 2 * LANES), F32),
        pltpu.VMEM((n, 8, LANES), BF16),
        pltpu.VMEM((n, 8, LANES), BF16),
        pltpu.VMEM((tp_n, ROWS, TP_PAD), F32),
        pltpu.VMEM((tp_n, ROWS, TP_PAD), F32),
        pltpu.VMEM((tp_n, ROWS, TP_PAD), F32),
        pltpu.VMEM((tp_n, ROWS, TP_PAD), F32),
        pltpu.VMEM((8 * SPAD, LANES), F32),
        pltpu.VMEM((8 * SPAD, LANES), F32),
        pltpu.VMEM((ROWS, TP_COLS), F32),
        pltpu.VMEM((quad_n, block, 2 * LANES), BF16),
        pltpu.VMEM((quad_n, block, 2 * LANES), BF16),
        pltpu.VMEM((quad_n, 32, block), F32),
        pltpu.VMEM((quad_n, 32, block), BF16),
        pltpu.VMEM((2, slots, 8, LANES), F32),
        pltpu.VMEM((n * 8, LANES), F32),
        pltpu.SemaphoreType.DMA((len(LOCAL),)),
        pltpu.SemaphoreType.DMA((5,)),
        pltpu.SemaphoreType.DMA((5,)),
        pltpu.SemaphoreType.DMA((max(1, depth_of(n) - 1),)),
    ]

    def step(*refs):
        kernel(n, tp_n, slots, *refs)

    layer, state = pl.pallas_call(
        step,
        out_shape=(
            jax.ShapeDtypeStruct((ROWS, TP_COLS), BF16),
            jax.ShapeDtypeStruct(scan_state.shape, F32),
        ),
        in_specs=[pl.BlockSpec(memory_space=pltpu.HBM)] * len(operand),
        out_specs=(pl.BlockSpec(memory_space=pltpu.VMEM),) * 2,
        scratch_shapes=scratch,
        compiler_params=pltpu.CompilerParams(collective_id=0, has_side_effects=True, vmem_limit_bytes=24 << 20),
        name="decode_layer",
    )(*operand)
    results = (jax.ShapeDtypeStruct(layer.shape, BF16), jax.ShapeDtypeStruct(state.shape, F32))
    return pl.pallas_call(
        write_out,
        out_shape=results,
        in_specs=[pl.BlockSpec(memory_space=pltpu.VMEM)] * 2,
        out_specs=(pl.BlockSpec(memory_space=pl.ANY),) * 2,
        scratch_shapes=[pltpu.SemaphoreType.DMA((2,))],
        compiler_params=pltpu.CompilerParams(vmem_limit_bytes=1 << 20),
        name="write_out",
    )(layer, state)


def solution(mesh):
    return jax.shard_map(
        body,
        mesh=mesh,
        in_specs=(
            P("req", None),
            P(),
            P(None, "tp"),
            P(None, "tp"),
            P("tp", None),
            P("tp"),
            P(None, None, "tp"),
            P(None, "tp"),
            P("req", None, "tp"),
            P("tp", None),
            P(None, "tp"),
            P("tp"),
            P(None, "tp"),
            P("tp"),
            P("req", None, "tp"),
            P("tp"),
            P("tp", None),
            P("req", "tp", None, None),
            P(),
            P("req"),
            P("req"),
        ),
        out_specs=(P("req", "tp"), P("req", None, "tp")),
        check_vma=False,
    )
```

```python
import math

import jax
import jax.numpy as jnp
import numpy as np
from jax import lax
from jax.experimental import pallas as pl
from jax.experimental.pallas import tpu as pltpu
from jax.sharding import PartitionSpec as P

F32 = jnp.float32
BF16 = jnp.bfloat16
NEG = -1e30
ROWS = 8
HEADS = 5
HD = 64
LANES = 128
SPAD = 40
TP_COLS = 400
TP_PAD = 512
NT = (((1,), (1,)), ((), ()))


def depth_of(n):
    return 8 if n >= 32 else n // 4


def iota(shape, axis):
    return lax.broadcasted_iota(jnp.int32, shape, axis)


def dot(a, b):
    return jnp.dot(a, b, preferred_element_type=F32)


def dot_nt(a, b):
    return lax.dot_general(a, b, NT, preferred_element_type=F32)


def silu(v):
    return v * (1.0 / (1.0 + jnp.exp(-v)))


def softplus(v):
    return jnp.maximum(v, 0.0) + jnp.log1p(jnp.exp(-jnp.abs(v)))


LOCAL = (
    "len_s", "sr_s", "sb_s", "hidden", "gain", "freq", "wq", "wm", "mi", "cw", "cs", "sw", "st", "sb", "dl", "sg",
    "ss", "mg", "mo", "cache", "ag", "wo",
)


def kernel(n, tp_n, slots, *refs):
    hbm = dict(zip(LOCAL, refs[: len(LOCAL)]))
    out_layer, out_state = refs[len(LOCAL) : len(LOCAL) + 2]
    refs = refs[len(LOCAL) + 2 :]
    ref = dict(zip(LOCAL, refs[: len(LOCAL)]))
    (
        q_all, sel_buf, msg, inbox, m_send, m_recv, a_send, a_recv, q_slot, o_slot, y_v,
        keys, values, scores_v, weights_v, stat_v, pick,
        in_sem, send_sem, recv_sem, z_sem,
    ) = refs[len(LOCAL) :]
    me = lax.axis_index("req")
    tp = lax.axis_index("tp")

    z_n = depth_of(n)
    plane_n = n // z_n
    x_n = plane_n // 2
    core = lax.rem(me, 2)
    z = lax.rem(lax.div(me, 2), z_n)
    x = lax.div(me, 2 * z_n)

    def ahead(at, by, count, stride):
        return jnp.where(at >= count - by, (by - count) * stride, by * stride) if by else 0

    z_order = sorted(range(1, z_n), key=lambda i: (min(i, z_n - i), i))
    z_step = {i: ahead(z, i, z_n, 2) for i in range(z_n)}
    column = {i: me + z_step[i] for i in z_order}
    x_step = {i: ahead(x, i, x_n, 2 * z_n) for i in range(x_n)}
    core_step = {0: 0, 1: 1 - 2 * core}
    plane_order = sorted(range(1, plane_n), key=lambda j: -min(j // 2, x_n - j // 2))
    plane_step = [x_step[j // 2] + core_step[j % 2] for j in plane_order]
    plane = [me + step for step in plane_step]
    tp_peer = [tp + ahead(tp, i, tp_n, 1) for i in sorted(range(1, tp_n), key=lambda i: -min(i, tp_n - i))]

    barrier = pltpu.get_barrier_semaphore()
    for i in reversed(z_order):
        pl.semaphore_signal(barrier, inc=1, device_id={"req": column[i]})
    for d in plane:
        pl.semaphore_signal(barrier, inc=1, device_id={"req": d})
    for p in tp_peer:
        pl.semaphore_signal(barrier, inc=1, device_id={"tp": p})
    copies = {}
    for k, name in enumerate(LOCAL):
        dst = ref[name].at[pl.ds(0, HEADS * HD)] if name == "wq" else ref[name]
        copies[name] = pltpu.make_async_copy(hbm[name], dst, in_sem.at[k])
        copies[name].start()

    inbox[...] = jnp.zeros_like(inbox)
    o_slot[...] = jnp.zeros_like(o_slot)
    q_slot[...] = jnp.zeros_like(q_slot)
    block = ref["cache"].shape[1]
    quad_n = (slots + 3) // 4

    def tp_start(src, dst, k):
        for p in tp_peer:
            pltpu.make_async_remote_copy(
                src_ref=src(p), dst_ref=dst.at[tp], send_sem=send_sem.at[k], recv_sem=recv_sem.at[k],
                device_id={"tp": p},
            ).start()

    def wait_all(buf, k, count, which):
        view = buf.at[pl.ds(0, count), pl.ds(0, 6)] if k == 3 else buf.at[pl.ds(0, count)]
        copy = pltpu.make_async_remote_copy(
            src_ref=view, dst_ref=view, send_sem=send_sem.at[k], recv_sem=recv_sem.at[k], device_id={"tp": tp}
        )
        if which == "send":
            copy.wait_send()
        else:
            copy.wait_recv()

    lane8 = iota((ROWS, LANES), 1)
    low8 = lane8 < HD

    ref["wq"][pl.ds(HEADS * HD, 64), :] = jnp.zeros((64, ref["wq"].shape[1]), BF16)
    copies["hidden"].wait()
    copies["gain"].wait()
    hidden = ref["hidden"][...].astype(F32)
    width = hidden.shape[1]
    mean = jnp.sum(hidden * hidden, axis=1, keepdims=True) * (1.0 / width)
    normed = (hidden * lax.rsqrt(mean + 1e-06) * ref["gain"][...].reshape(1, width)).astype(BF16)

    for name in ("len_s", "sr_s", "sb_s", "freq"):
        copies[name].wait()
    position = jnp.zeros((ROWS, LANES), F32)
    row8 = iota((ROWS, LANES), 0)
    for r in range(ROWS):
        position = jnp.where(row8 == r, ref["len_s"][me * ROWS + r].astype(F32), position)
    angles = position * ref["freq"][...]
    cosine = jnp.cos(angles)
    sine = jnp.sin(angles)
    front = (lane8 & (HD - 1)) < HD // 2

    def rot(v):
        other = jnp.where(front, -pltpu.roll(v, LANES - HD // 2, 1), pltpu.roll(v, HD // 2, 1))
        return v * cosine + other * sine

    copies["wq"].wait()
    q_raw = dot_nt(normed, ref["wq"][...])
    query = [rot(q_raw[:, c * LANES : (c + 1) * LANES]).astype(BF16) for c in range(3)]
    for c in range(3):
        q_all[me, :, c * LANES : (c + 1) * LANES] = query[c]

    pl.semaphore_wait(barrier, len(z_order) + len(plane) + tp_n - 1)

    def z_copy(i, source, target):
        return pltpu.make_async_remote_copy(
            src_ref=q_all.at[source], dst_ref=q_all.at[source], send_sem=send_sem.at[0], recv_sem=z_sem.at[i - 1],
            device_id={"req": target},
        )

    def pass_on(source):
        for d in plane:
            pltpu.make_async_remote_copy(
                src_ref=q_all.at[source], dst_ref=q_all.at[source], send_sem=send_sem.at[0], recv_sem=recv_sem.at[0],
                device_id={"req": d},
            ).start()

    def pass_on_from(distance):
        for i in z_order:
            if min(i, z_n - i) == distance:
                source = column[z_n - i]
                z_copy(i, source, source).wait_recv()
                pass_on(source)

    for i in reversed(z_order):
        z_copy(i, me, column[i]).start()
    pass_on(me)

    copies["mi"].wait()
    mamba_x = dot_nt(normed, ref["mi"][0]).astype(BF16)
    for name in ("cw", "cs", "sw"):
        copies[name].wait()
    taps = ref["cw"].shape[0]
    conv = ref["cw"][taps - 1 : taps, :] * mamba_x.astype(F32)
    for j in range(taps - 1):
        conv = conv + ref["cw"][j : j + 1, :] * ref["cs"][j].astype(F32)
    activated = silu(conv).astype(BF16)
    part = dot_nt(activated, ref["sw"][...])
    sel_buf[tp] = jnp.concatenate([part, jnp.zeros((ROWS, 2 * LANES - part.shape[1]), F32)], axis=1)
    tp_start(lambda p: sel_buf.at[tp], sel_buf, 1)

    def pack(quads):
        for g in quads:
            for c in range(2):
                s0 = 4 * g + 2 * c
                lanes = slice(c * LANES, (c + 1) * LANES)
                if s0 < slots:
                    one, two = ref["cache"][s0], ref["cache"][s0 + 1]
                    keys[g, :, lanes] = jnp.concatenate([one[:, 0:HD], two[:, 0:HD]], axis=1)
                    values[g, :, lanes] = jnp.concatenate([one[:, HD:], two[:, HD:]], axis=1)

    pass_on_from(1)
    copies["cache"].wait()
    third = quad_n // 3
    pack(range(0, third))
    for distance in range(2, z_n // 2 + 1):
        pass_on_from(distance)
    pack(range(third, quad_n))
    lane40 = lax.rem(lane8, SPAD)
    lane40 = jnp.where(lane8 < 3 * SPAD, lane40, -1)
    sr_row = jnp.full((ROWS, LANES), -1, jnp.int32)
    sub_col = iota((SPAD, LANES), 0)
    sr_col = jnp.full((SPAD, LANES), -1, jnp.int32)
    for s in range(slots):
        v = ref["sr_s"][s]
        sr_row = jnp.where(lane40 == s, v, sr_row)
        sr_col = jnp.where(sub_col == s, v, sr_col)
    dest_row = lax.shift_right_arithmetic(sr_row, 3)
    rank_row = jnp.zeros((ROWS, LANES), jnp.int32)
    for s in range(slots):
        d = lax.shift_right_arithmetic(ref["sr_s"][s], 3)
        rank_row = rank_row + jnp.where((dest_row == d) & (lane40 > s), 1, 0)
    mr = iota((8, LANES), 0)
    cj = jnp.where(lane8 < SPAD, 0, jnp.where(lane8 < 2 * SPAD, 1, jnp.where(lane8 < 3 * SPAD, 2, -1)))
    fits = ((mr & 1) == rank_row) & (lax.shift_right_arithmetic(mr, 1) == cj)
    dests = [me + (z_step[i] + step) for i in list(reversed(z_order)) + [0] for step in plane_step + [0]]
    for k, d in enumerate(dests):
        pick[k * 8 : (k + 1) * 8, :] = jnp.where(fits & (dest_row == d), 1.0, 0.0)
    own_pick = jnp.concatenate([sr_col] * (n * 8 // LANES), axis=1) if n * 8 >= LANES else sr_col[:, 0 : n * 8]
    own_pick = jnp.where(own_pick == iota((SPAD, n * 8), 1), 1.0, 0.0).astype(BF16)

    wait_all(q_all, 0, n - z_n, "recv")
    q_sel = dot(own_pick, q_all[...].reshape(n * 8, 3 * LANES))
    low40 = iota((SPAD, LANES), 1) < HD
    for h in range(HEADS):
        col = q_sel[:, (h // 2) * LANES : (h // 2 + 1) * LANES]
        turn = pltpu.roll(col, HD, 1)
        both = jnp.where(low40, col, turn) if h % 2 == 0 else jnp.where(low40, turn, col)
        q_slot[h * SPAD : (h + 1) * SPAD, :] = both * HD**-0.5
    time = iota((8, block), 1)

    def live(s):
        owner = ref["sr_s"][s]
        used = owner >= 0
        return jnp.where(used, ref["len_s"][jnp.where(used, owner, 0)] - ref["sb_s"][s] * block, 0)

    zero = jnp.zeros((8, LANES), F32)
    for g in range(quad_n):
        held = min(4, slots - 4 * g)
        lhs = []
        for i in range(held):
            q = q_slot[pl.ds(4 * g + i, 8, stride=SPAD), :]
            q = jnp.where(low8, q, 0.0) if i % 2 == 0 else jnp.where(low8, 0.0, q)
            lhs.append(q if held == 2 else jnp.concatenate([q, zero] if i < 2 else [zero, q], axis=1))
        lhs = jnp.concatenate(lhs, axis=0).astype(BF16)
        scores_v[g, 0 : 8 * held, :] = dot_nt(lhs, keys[g, :, 0 : HD * held])
    for g in range(quad_n):
        for i in range(4):
            s = 4 * g + i
            rows = slice(i * 8, i * 8 + 8)
            if s >= slots:
                continue
            scores = jnp.where(time < live(s), scores_v[g, rows, :], NEG)
            top = jnp.max(scores, axis=1, keepdims=True)
            weights = jnp.exp(scores - top).astype(BF16)
            weights_v[g, rows, :] = weights
            total = jnp.sum(weights.astype(F32), axis=1, keepdims=True)
            stat_v[0, s] = jnp.broadcast_to(top + jnp.log(total), (8, LANES))
            stat_v[1, s] = jnp.broadcast_to(1.0 / total, (8, LANES))
    for g in range(quad_n):
        held = min(4, slots - 4 * g)
        out = dot(weights_v[g, 0 : 8 * held, :], values[g, :, 0 : HD * held])
        for i in range(4):
            s = 4 * g + i
            if s < slots:
                part = out[i * 8 : i * 8 + 8, (i // 2) * LANES : (i // 2 + 1) * LANES] * stat_v[1, s]
                lse = stat_v[0, s]
                part = jnp.where(low8, part, lse) if i % 2 == 0 else jnp.where(low8, lse, part)
                o_slot[pl.ds(s, 8, stride=SPAD), :] = part

    lane40v = iota((SPAD, LANES), 1)
    odd = (iota((SPAD, LANES), 0) & 1) == 1
    outs, turned = [], []
    for h in range(HEADS):
        one = o_slot[h * SPAD : (h + 1) * SPAD, :]
        two = pltpu.roll(one, HD, 1)
        outs.append(jnp.where(odd, one, two))
        turned.append(jnp.where(odd, two, one))
    tail = jnp.where(lane40v == 80, ((sr_col & 7) + 1).astype(F32), 0.0)
    for h in range(HEADS):
        rest = turned[h]
        for t in range(3):
            term = rest.astype(BF16).astype(F32)
            tail = jnp.where(lane40v == HD + 3 * h + t, term, tail)
            rest = rest - term
    table = jnp.concatenate(
        [
            jnp.where(low40, turned[0], outs[1]),
            jnp.where(low40, turned[2], outs[3]),
            jnp.where(low40, turned[4], tail),
            jnp.zeros((8, LANES), F32),
        ],
        axis=0,
    ).astype(BF16)
    part_n = n // 4
    for c in range(4):
        rows = pick[c * part_n * 8 : (c + 1) * part_n * 8, :].astype(BF16)
        msg[c * part_n : (c + 1) * part_n] = dot(rows, table).reshape(part_n, 8, LANES).astype(BF16)
        for k in range(c * part_n, min((c + 1) * part_n, n - 1)):
            pltpu.make_async_remote_copy(
                src_ref=msg.at[k, pl.ds(0, 6)], dst_ref=inbox.at[me, pl.ds(0, 6)], send_sem=send_sem.at[3],
                recv_sem=recv_sem.at[3], device_id={"req": dests[k]},
            ).start()
    inbox[me] = msg[n - 1]

    gate = silu(dot_nt(normed, ref["mi"][1]))
    copies["wm"].wait()
    memory = dot(normed, ref["wm"][...])
    key_value = jnp.where(low8, rot(memory), memory).astype(BF16).astype(F32)
    swapped = pltpu.roll(key_value, HD, 1)
    key_both = jnp.where(low8, key_value, swapped)
    value_both = jnp.where(low8, swapped, key_value)

    own_score = []
    for h in range(HEADS):
        half = low8 if h % 2 == 0 else jnp.logical_not(low8)
        prod = jnp.where(half, query[h // 2].astype(F32) * key_both, 0.0)
        own_score.append(jnp.sum(prod, axis=1, keepdims=True) * HD**-0.5)

    wait_all(sel_buf, 1, tp_n - 1, "recv")
    selection = sel_buf[0]
    for p in range(1, tp_n):
        selection = selection + sel_buf[p]
    dtr = ref["st"].shape[1]
    ns = ref["dl"].shape[0]
    for name in ("st", "sb", "dl", "sg", "ss", "mg", "mo"):
        copies[name].wait()
    step = softplus(dot_nt(selection[:, 0:dtr].astype(BF16), ref["st"][...]) + ref["sb"][...])
    maps = pltpu.roll(selection, selection.shape[1] - dtr, 1)[:, 0:LANES]
    maps = jnp.transpose(maps)
    active = activated.astype(F32)
    decay = jnp.exp(ref["dl"][...])
    drive = step * active
    for r in range(ROWS):
        new = (
            jnp.exp(-step[r : r + 1, :] * decay) * ref["ss"][r]
            + drive[r : r + 1, :] * maps[0:ns, r : r + 1]
        )
        out_state[r] = new
        y_v[r : r + 1, :] = jnp.sum(maps[ns : 2 * ns, r : r + 1] * new, axis=0, keepdims=True)
    mamba_y = (y_v[...] + ref["sg"][...] * active) * gate

    def share(used, weight, square, send, recv, k):
        proj = dot(used, weight)
        extra = jnp.zeros((ROWS, 13 * LANES - proj.shape[1]), F32)
        proj = jnp.concatenate([proj, extra], axis=1)
        lane = iota((ROWS, TP_PAD), 1)
        terms, remain = jnp.zeros((ROWS, TP_PAD), F32), square
        for k_term in range(3):
            term = remain.astype(BF16).astype(F32)
            terms = jnp.where(lane == TP_COLS + k_term, term, terms)
            remain = remain - term
        for p in range(tp_n):
            moved = proj if p == 0 else pltpu.roll(proj, proj.shape[1] - p * TP_COLS, 1)
            send[p] = jnp.where(lane >= TP_COLS, terms, moved[:, 0:TP_PAD]).astype(send.dtype)
        recv[tp] = send[tp]
        tp_start(lambda p: send.at[p], recv, k)

    def gathered(recv, k):
        wait_all(recv, k, tp_n - 1, "recv")
        total = recv[0].astype(F32)
        for p in range(1, tp_n):
            total = total + recv[p].astype(F32)
        square = total[:, TP_COLS : TP_COLS + 1]
        for k_term in range(1, 3):
            square = square + total[:, TP_COLS + k_term : TP_COLS + k_term + 1]
        return total, square

    mamba_square = jnp.sum(mamba_y * mamba_y, axis=1, keepdims=True)
    share((mamba_y * ref["mg"][...]).astype(BF16), ref["mo"][...], mamba_square, m_send, m_recv, 2)

    wide = jnp.concatenate([hidden, jnp.zeros((ROWS, 13 * LANES - width), F32)], axis=1)
    residual = wide[:, 0:TP_PAD]
    for p in range(1, tp_n):
        residual = jnp.where(tp == p, pltpu.roll(wide, wide.shape[1] - p * TP_COLS, 1)[:, 0:TP_PAD], residual)
    e_row = iota((16, LANES), 0)
    e_lane = iota((16, LANES), 1)
    e_start = HD + 3 * e_row
    spread_rows = ((e_row < HEADS) & (e_lane >= e_start) & (e_lane < e_start + 3)) | ((e_row == HEADS) & (e_lane == 80))
    spread_rows = jnp.where(spread_rows, 1.0, 0.0).astype(BF16)
    copies["ag"].wait()
    copies["wo"].wait()

    wait_all(inbox, 3, n - 1, "recv")
    box = inbox[...].reshape(n * 8, LANES)
    heads_row = dot_nt(spread_rows, box)
    col_j = lax.shift_right_arithmetic(iota((ROWS, n * 8), 1) & 7, 1)
    r_id = (iota((ROWS, n * 8), 0) + 1).astype(F32)
    shifted = [pltpu.roll(heads_row, n * 8 - (4 - 2 * j), 1) if j < 2 else heads_row for j in range(3)]
    high, low, den, own_w = [], [], [], []
    for h in range(HEADS):
        j = h // 2
        lse = jnp.broadcast_to(shifted[j][h : h + 1, :], (ROWS, n * 8))
        rid = jnp.broadcast_to(shifted[j][HEADS : HEADS + 1, :], (ROWS, n * 8))
        mine = (rid == r_id) & (col_j == j)
        top = jnp.maximum(jnp.max(jnp.where(mine, lse, NEG), axis=1, keepdims=True), own_score[h])
        w = jnp.where(mine, jnp.exp(lse - top), 0.0)
        own = jnp.exp(own_score[h] - top)
        den.append(jnp.sum(w, axis=1, keepdims=True) + own)
        own_w.append(own)
        w_high = w.astype(BF16).astype(F32)
        high.append(w_high)
        low.append(w - w_high)
    merged = dot(jnp.concatenate(high + low, axis=0).astype(BF16), box)
    numer = [
        merged[h * 8 : h * 8 + 8] + merged[(HEADS + h) * 8 : (HEADS + h) * 8 + 8] + own_w[h] * value_both
        for h in range(HEADS)
    ]
    normal = [numer[h] / den[h] for h in range(HEADS)]
    attention = jnp.concatenate(
        [
            jnp.where(low8, normal[0], normal[1]),
            jnp.where(low8, normal[2], normal[3]),
            jnp.where(low8, normal[4], 0.0),
        ],
        axis=1,
    )[:, 0 : HEADS * HD]
    attn_square = jnp.sum(attention * attention, axis=1, keepdims=True)
    share((attention * ref["ag"][...].reshape(1, HEADS * HD)).astype(BF16), ref["wo"][...], attn_square, a_send, a_recv, 4)
    mamba, square = gathered(m_recv, 2)
    mamba_scale = jnp.sqrt(square * (1.0 / (TP_COLS * tp_n)) + 1e-06)
    base = residual + 0.5 * (mamba / mamba_scale)
    attn, square = gathered(a_recv, 4)
    attn_scale = jnp.sqrt(square * (1.0 / (HEADS * HD * tp_n)) + 1e-06)
    final = base + 0.5 * (attn / attn_scale)
    out_layer[...] = final[:, 0:TP_COLS].astype(BF16)
    wait_all(q_all, 0, n - 1, "send")
    wait_all(sel_buf, 1, tp_n - 1, "send")
    wait_all(m_send, 2, tp_n - 1, "send")
    wait_all(msg, 3, n - 1, "send")
    wait_all(a_send, 4, tp_n - 1, "send")


def write_out(layer, state, layer_out, state_out, sem):
    first = pltpu.make_async_copy(state, state_out, sem.at[0])
    second = pltpu.make_async_copy(layer, layer_out, sem.at[1])
    first.start()
    second.start()
    first.wait()
    second.wait()


def body(
    hidden_in, norm_gain, query_weight, memory_weight, attention_out, attention_gain, mamba_input, conv_weight,
    conv_state, select_weight, step_weight, step_bias, decay_log, skip_gain, scan_state, mamba_gain, mamba_out,
    cache_blocks, lengths, slot_request, slot_block,
):
    n = lax.axis_size("req")
    tp_n = lax.axis_size("tp")
    slots, _, block, kv = cache_blocks.shape
    quad_n = (slots + 3) // 4
    rate = 10000.0 ** (-(np.arange(LANES) % (HD // 2)) * (2.0 / HD))
    freq = jnp.asarray(np.broadcast_to(rate[None, :], (ROWS, LANES)), F32)
    row = lambda v: v.reshape(1, -1)
    operand = {
        "len_s": lengths,
        "sr_s": slot_request,
        "sb_s": slot_block,
        "hidden": hidden_in,
        "gain": norm_gain,
        "freq": freq,
        "wq": query_weight.T,
        "wm": memory_weight,
        "mi": jnp.transpose(mamba_input, (0, 2, 1)),
        "cw": conv_weight,
        "cs": jnp.transpose(conv_state, (1, 0, 2)),
        "sw": select_weight.T,
        "st": step_weight.T,
        "sb": row(step_bias),
        "dl": decay_log,
        "sg": row(skip_gain),
        "ss": scan_state,
        "mg": row(mamba_gain),
        "mo": mamba_out,
        "cache": cache_blocks.reshape(slots, block, kv),
        "ag": attention_gain,
        "wo": attention_out,
    }
    operand = [pltpu.with_memory_space_constraint(operand[name], pltpu.HBM) for name in LOCAL]
    scratch = []
    for name, v in zip(LOCAL, operand):
        space = pltpu.SMEM if name in ("len_s", "sr_s", "sb_s") else pltpu.VMEM
        shape = (v.shape[0] + 64, v.shape[1]) if name == "wq" else v.shape
        scratch.append(space(shape, v.dtype))
    scratch += [
        pltpu.VMEM((n, ROWS, 3 * LANES), BF16),
        pltpu.VMEM((tp_n, ROWS, 2 * LANES), F32),
        pltpu.VMEM((n, 8, LANES), BF16),
        pltpu.VMEM((n, 8, LANES), BF16),
        pltpu.VMEM((tp_n, ROWS, TP_PAD), F32),
        pltpu.VMEM((tp_n, ROWS, TP_PAD), F32),
        pltpu.VMEM((tp_n, ROWS, TP_PAD), F32),
        pltpu.VMEM((tp_n, ROWS, TP_PAD), F32),
        pltpu.VMEM((8 * SPAD, LANES), F32),
        pltpu.VMEM((8 * SPAD, LANES), F32),
        pltpu.VMEM((ROWS, TP_COLS), F32),
        pltpu.VMEM((quad_n, block, 2 * LANES), BF16),
        pltpu.VMEM((quad_n, block, 2 * LANES), BF16),
        pltpu.VMEM((quad_n, 32, block), F32),
        pltpu.VMEM((quad_n, 32, block), BF16),
        pltpu.VMEM((2, slots, 8, LANES), F32),
        pltpu.VMEM((n * 8, LANES), F32),
        pltpu.SemaphoreType.DMA((len(LOCAL),)),
        pltpu.SemaphoreType.DMA((5,)),
        pltpu.SemaphoreType.DMA((5,)),
        pltpu.SemaphoreType.DMA((max(1, depth_of(n) - 1),)),
    ]

    def step(*refs):
        kernel(n, tp_n, slots, *refs)

    layer, state = pl.pallas_call(
        step,
        out_shape=(
            jax.ShapeDtypeStruct((ROWS, TP_COLS), BF16),
            jax.ShapeDtypeStruct(scan_state.shape, F32),
        ),
        in_specs=[pl.BlockSpec(memory_space=pltpu.HBM)] * len(operand),
        out_specs=(pl.BlockSpec(memory_space=pltpu.VMEM),) * 2,
        scratch_shapes=scratch,
        compiler_params=pltpu.CompilerParams(collective_id=0, has_side_effects=True, vmem_limit_bytes=24 << 20),
        name="decode_layer",
    )(*operand)
    results = (jax.ShapeDtypeStruct(layer.shape, BF16), jax.ShapeDtypeStruct(state.shape, F32))
    return pl.pallas_call(
        write_out,
        out_shape=results,
        in_specs=[pl.BlockSpec(memory_space=pltpu.VMEM)] * 2,
        out_specs=(pl.BlockSpec(memory_space=pl.ANY),) * 2,
        scratch_shapes=[pltpu.SemaphoreType.DMA((2,))],
        compiler_params=pltpu.CompilerParams(vmem_limit_bytes=1 << 20),
        name="write_out",
    )(layer, state)


def solution(mesh):
    return jax.shard_map(
        body,
        mesh=mesh,
        in_specs=(
            P("req", None),
            P(),
            P(None, "tp"),
            P(None, "tp"),
            P("tp", None),
            P("tp"),
            P(None, None, "tp"),
            P(None, "tp"),
            P("req", None, "tp"),
            P("tp", None),
            P(None, "tp"),
            P("tp"),
            P(None, "tp"),
            P("tp"),
            P("req", None, "tp"),
            P("tp"),
            P("tp", None),
            P("req", "tp", None, None),
            P(),
            P("req"),
            P("req"),
        ),
        out_specs=(P("req", "tp"), P("req", None, "tp")),
        check_vma=False,
    )
```
